32 devices in a mesh: row: 16 (over z, x, core), col: 2 (over y).
Axes of the slice: x: 2, y: 2, z: 4, core: 2. Of those that a mesh axis runs over, the one named last changes fastest.
Arguments:
- inverse_anc: float32 [8192, 8192], P('row', 'col'), as said below
- lower_panel: float32 [8192, 512], P('row', 'col'), may hold values from -0.5 to 0.5
- structure: int32 [2, 16], P('col'), may hold values from 0 to 31, as said below
- diag_inverse: float32 [512, 256], P('col'), may hold values from -6 to 6
Outputs:
- inverse_panel: float32 [8192, 512], P('row', 'col')
- diagonal_block: float32 [512, 256], P('col')
The draws below stay inside these ranges and needn't reach their ends.
Inputs may be any that keep to these rules, and one draw needn't show every extreme that they name: inverse_anc is exactly symmetric. `structure`: each row lists 16 different ancestor block numbers in increasing order; each index of col holds exactly one row (one lower supernode).
All inputs are finite; a program needn't handle non-finite values.
Results may differ from the reference program's by a relative error of at most 0.000075.
Values sent between devices are 32-bit elements; how exact they have to be, the bound alone decides.
No kernel may reach another device: no remote copies, remote signals or barrier semaphores. Data moves between devices by JAX's collectives and lax.ppermute only.
A program may use at most 64 MiB of HBM per device.

```python
import math
import jax
import jax.numpy as jnp
from jax import lax

B = 256
ANC = 32
STR = 16
SN_DEV = 1
NS = 2
ORDER = 8192


def draw_inverse_anc(key, part):
    matrix_order = ANC * B
    key_first = jax.random.fold_in(jax.random.fold_in(key, 11), 0)
    normal_base = jax.random.normal(key_first, (matrix_order, matrix_order), jnp.float32)
    symmetric = (normal_base + normal_base.T) / math.sqrt(2.0 * matrix_order)
    return symmetric + jnp.eye(matrix_order, dtype=jnp.float32)


def draw_structure(key, part):
    groups = NS // SN_DEV
    rounds = (SN_DEV * STR + ANC - 1) // ANC
    positions = jnp.arange(ANC, dtype=jnp.int32)
    scores = jax.random.randint(jax.random.fold_in(key, 7), (groups, rounds, ANC), 0, 1048576, dtype=jnp.int32)
    scores = scores * ANC + positions[None, None, :]
    orders = jnp.argsort(scores, axis=2).astype(jnp.int32)
    supernodes = jnp.arange(NS, dtype=jnp.int32)
    group_ids = supernodes // SN_DEV
    slot_ids = supernodes % SN_DEV
    round_ids = slot_ids * STR // ANC
    offsets = slot_ids * STR % ANC
    columns = offsets[:, None] + jnp.arange(STR, dtype=jnp.int32)[None, :]
    picked = orders[group_ids[:, None], round_ids[:, None], columns]
    return jnp.sort(picked, axis=1).astype(jnp.int32)


def level_of(stream_key, dims, shards, low, high):
    factor_of, own = 1.0, jax.random.fold_in(stream_key, 6)
    for axis_at, parts in shards:
        heights = jnp.exp(jax.random.uniform(jax.random.fold_in(own, axis_at), (parts,), jnp.float32, low / len(shards), high / len(shards)))
        factor_of = factor_of * jnp.repeat(heights, dims[axis_at] // parts).reshape([-1 if axis == axis_at else 1 for axis in range(len(dims))])
    return factor_of


def bell_draw(stream_key, shape, spread, bound, shards=(), kind=jnp.bfloat16):
    gain = level_of(stream_key, shape, shards, -0.22, 0.18) if shards else 1.0
    entries = jax.random.normal(stream_key, shape, jnp.float32) * spread * gain
    return jnp.minimum(jnp.maximum(entries, -bound), bound).astype(kind)


def setup_inputs(seed: int = 0) -> dict:
    keys = jax.random.split(jax.random.key(seed), 5)
    return {
        "inverse_anc": draw_inverse_anc(jax.random.fold_in(keys[4], 71), 0),
        "lower_panel": bell_draw(keys[1], (ORDER, NS * B), 0.0625, 0.5, ((0, 16), (1, 2)), jnp.float32),
        "structure": draw_structure(jax.random.fold_in(keys[4], 71), 0),
        "diag_inverse": bell_draw(keys[3], (NS * B, B), 1.0, 6.0, ((0, 2),), jnp.float32),
    }


def keep_rows(structure, first_row, row_count, sn_width):
    block_ids = (first_row + jnp.arange(row_count, dtype=jnp.int32)) // sn_width
    listed = jnp.any(structure[None, :, :] == block_ids[:, None, None], axis=2)
    return jnp.repeat(listed, sn_width, axis=1)


def reference(inverse_anc, lower_panel, structure, diag_inverse):
    matrix_order = inverse_anc.shape[0]
    keep_mask = keep_rows(structure, jnp.int32(0), matrix_order, B)
    masked = jnp.where(keep_mask, lower_panel, jnp.float32(0.0))
    product = jnp.dot(inverse_anc, masked, precision=lax.Precision.HIGHEST, preferred_element_type=jnp.float32)
    panel = jnp.where(keep_mask, -product, jnp.float32(0.0))
    lower_blocks = masked.reshape(matrix_order, NS, B)
    panel_blocks = panel.reshape(matrix_order, NS, B)
    terms = jnp.einsum("ika,ikb->kab", lower_blocks, panel_blocks, precision=lax.Precision.HIGHEST)
    return panel, diag_inverse - terms.reshape(NS * B, B)
```

```python
import functools

import jax
import jax.numpy as jnp
from jax import lax
from jax.experimental import pallas as pl
from jax.experimental.pallas import tpu as pltpu
from jax.sharding import PartitionSpec as P

BOTH = ("row", "col")


def keep_rows(structure, first_row, row_count, sn_width):
    block_ids = (first_row + jnp.arange(row_count, dtype=jnp.int32)) // sn_width
    listed = jnp.any(structure[None, :, :] == block_ids[:, None, None], axis=2)
    return jnp.repeat(listed, sn_width, axis=1)


def local_any(inverse_anc, lower_panel, structure, diag_inverse):
    local_rows = inverse_anc.shape[0]
    sn_width = diag_inverse.shape[1]
    local_count = structure.shape[0]
    keep = keep_rows(structure, lax.axis_index("row") * local_rows, local_rows, sn_width)
    masked = jnp.where(keep, lower_panel, jnp.float32(0.0))
    rows = lax.all_gather(masked, "row", axis=0, tiled=True)
    rows = lax.all_to_all(rows, "col", split_axis=0, concat_axis=1, tiled=True)
    part = jnp.dot(inverse_anc, rows, precision=lax.Precision.HIGHEST)
    product = lax.psum_scatter(part, "col", scatter_dimension=1, tiled=True)
    panel = jnp.where(keep, -product, jnp.float32(0.0))
    terms = jnp.einsum(
        "ika,ikb->kab",
        masked.reshape(local_rows, local_count, sn_width),
        panel.reshape(local_rows, local_count, sn_width),
        precision=lax.Precision.HIGHEST,
    )
    total = lax.psum(terms.reshape(local_count * sn_width, sn_width), "row")
    return panel, diag_inverse - total


def split(value):
    high = value.astype(jnp.bfloat16)
    low = (value - high.astype(jnp.float32)).astype(jnp.bfloat16)
    return high, low


def dot3(a, b, dims):
    dot = lambda u, v: lax.dot_general(u, v, (dims, ((), ())), preferred_element_type=jnp.float32)
    return dot(a[0], b[0]) + (dot(a[0], b[1]) + dot(a[1], b[0]))


def product_kernel(slots, blocks, width, has_acc, final, table, *refs):
    count = len(slots)
    narrays = 1 + max(s[0] for s in slots)
    refs = list(refs)
    a_hbm = refs.pop(0)
    arrays = [refs.pop(0) for _ in range(narrays)]
    acc_in = refs.pop(0) if has_acc else None
    if final:
        recv, lower = refs.pop(0), refs.pop(0)
    out = refs.pop(0)
    if final:
        terms = refs.pop(0)
    a_buf, p_buf, a_sem, p_sem = refs
    row_on = [table[2 * count + rb] > 0 for rb in range(blocks)]

    def a_copy(p, rb):
        return pltpu.make_async_copy(
            a_hbm.at[pl.ds(rb * width, width), pl.ds(pl.multiple_of(table[p] * width, width), width)],
            a_buf.at[p, rb],
            a_sem.at[p, rb],
        )

    def p_copy(p):
        array, at = slots[p]
        return pltpu.make_async_copy(arrays[array].at[pl.ds(at * width, width), :], p_buf.at[p], p_sem.at[p])

    for p in range(count):
        @pl.when(table[count + p] > 0)
        def _(p=p):
            p_copy(p).start()
            for rb in range(blocks):
                @pl.when(row_on[rb])
                def _(rb=rb):
                    a_copy(p, rb).start()

    if has_acc:
        out[...] = acc_in[...]
    else:
        out[...] = jnp.zeros_like(out)
    for p in range(count):
        @pl.when(table[count + p] > 0)
        def _(p=p):
            p_copy(p).wait()
            piece = split(p_buf[p])
            for rb in range(blocks):
                @pl.when(row_on[rb])
                def _(rb=rb):
                    a_copy(p, rb).wait()
                    out[pl.ds(rb * width, width), :] += dot3(split(a_buf[p, rb]), piece, ((1,), (0,)))

    if final:
        terms[...] = jnp.zeros_like(terms)
        for rb in range(blocks):
            rows = pl.ds(rb * width, width)

            @pl.when(row_on[rb])
            def _(rows=rows):
                panel = -(out[rows, :] + recv[rows, :])
                out[rows, :] = panel
                terms[...] += dot3(split(lower[rows, :]), split(panel), ((0,), (0,)))

            @pl.when(jnp.logical_not(row_on[rb]))
            def _(rows=rows):
                out[rows, :] = jnp.zeros((width, out.shape[1]), jnp.float32)


def product(table, inverse_anc, arrays, slots, width, acc=None, final=None):
    rows = inverse_anc.shape[0]
    blocks = rows // width
    count = len(slots)
    any_spec = pl.BlockSpec(memory_space=pl.ANY)
    vmem = pl.BlockSpec(memory_space=pltpu.VMEM)
    operands = [inverse_anc, *arrays]
    specs = [any_spec] * len(operands)
    if acc is not None:
        operands.append(acc)
        specs.append(vmem)
    if final is not None:
        operands += list(final)
        specs += [vmem, vmem]
    shapes = [jax.ShapeDtypeStruct((rows, width), jnp.float32)]
    if final is not None:
        shapes.append(jax.ShapeDtypeStruct((width, width), jnp.float32))
    return pl.pallas_call(
        functools.partial(product_kernel, slots, blocks, width, acc is not None, final is not None),
        out_shape=shapes,
        grid_spec=pltpu.PrefetchScalarGridSpec(
            num_scalar_prefetch=1,
            grid=(1,),
            in_specs=specs,
            out_specs=[vmem] * len(shapes),
            scratch_shapes=[
                pltpu.VMEM((count, blocks, width, width), jnp.float32),
                pltpu.VMEM((count, width, width), jnp.float32),
                pltpu.SemaphoreType.DMA((count, blocks)),
                pltpu.SemaphoreType.DMA((count,)),
            ],
        ),
        cost_estimate=pl.CostEstimate(
            flops=6 * rows * width * width * count // 4,
            bytes_accessed=4 * rows * width * count // 2,
            transcendentals=0,
        ),
    )(table, *operands)


CORE, X, Z, FAR = 1, 2, 4, 8
FIRST = ([(0, 0), (0, 1), (1, 0), (1, 1), (2, 0), (3, 0), (4, 0), (5, 0)],
         [(0, 0), (0, 1), (1, 0), (1, 1), (2, 0), (3, 0), (4, 1), (5, 1)])
SECOND = ([(0, 0), (0, 1), (1, 0), (1, 1), (2, 0), (2, 1), (3, 0), (3, 1)],
          [(4, 0), (6, 0), (5, 0), (7, 0), (2, 1), (6, 1), (3, 1), (7, 1)])


def local_two(n_row, inverse_anc, lower_panel, structure, diag_inverse):
    n_col = 2
    rows = inverse_anc.shape[0]
    width = diag_inverse.shape[1]
    row, col = lax.axis_index("row"), lax.axis_index("col")
    near = (row // FAR) == col
    flip = [(0, 1), (1, 0)]

    def swap(value, mask):
        return lax.ppermute(value, "row", [(i, i ^ mask) for i in range(n_row)])

    def linear(r, c):
        return r * n_col + c

    every = [(r, c) for r in range(n_row) for c in range(n_col)]
    first = [
        (linear(r, c), linear(r ^ FAR, c) if r // FAR == c else linear(r, 1 - c)) for r, c in every
    ]
    second = [(linear(r, c), linear(r ^ FAR, 1 - c)) for r, c in every if r // FAR != c]
    got_first = lax.ppermute(lower_panel, BOTH, first)
    got_second = lax.ppermute(lower_panel, BOTH, second)
    other_structure = lax.ppermute(structure, "col", flip)
    q_own = jnp.where(near, lower_panel, got_first)
    q_other = jnp.where(near, got_first, got_second)

    def table(listed, order):
        block = ((row % FAR) ^ jnp.array([m for m, _ in order], jnp.int32)) * 2
        block = block + jnp.array([h for _, h in order], jnp.int32)
        ids = jnp.concatenate([block + col * 2 * FAR, row * 2 + jnp.arange(2, dtype=jnp.int32)])
        on = jnp.any(ids[:, None] == listed[0][None, :], axis=1).astype(jnp.int32)
        return jnp.concatenate([block, on])

    half = rows // 2

    def step_one(q):
        return swap(q[:half], X), swap(q[half:], Z)

    def step_two(q, xa, zb):
        return swap(jnp.concatenate([q[:half], xa]), Z), swap(jnp.concatenate([q[half:], zb]), X)

    sib = lambda v: swap(v, CORE)
    one_o = step_one(q_other)
    one_w = step_one(q_own)
    two_o = step_two(q_other, *one_o)
    two_w = step_two(q_own, *one_w)

    def groups(q, one, two):
        g1 = [q, sib(q), one[0], sib(one[0]), one[1], sib(one[1])]
        g2 = [two[0], sib(two[0]), two[1], sib(two[1])]
        return g1, g2

    o1, o2 = groups(q_other, one_o, two_o)
    w1, w2 = groups(q_own, one_w, two_w)
    slots1 = ((0, 0), (0, 1), (1, 0), (1, 1), (2, 0), (3, 0), (4, 0), (5, 0))
    slots2 = ((0, 0), (0, 1), (1, 0), (1, 1), (2, 0), (2, 1), (3, 0), (3, 1))
    (part,) = product(table(other_structure, FIRST[1]), inverse_anc, o1, slots1, width)
    (part,) = product(table(other_structure, SECOND[1]), inverse_anc, o2, slots2, width, acc=part)
    recv = lax.ppermute(part, "col", flip)
    (acc,) = product(table(structure, FIRST[1]), inverse_anc, w1, slots1, width)
    panel, terms = product(
        table(structure, SECOND[1]), inverse_anc, w2, slots2, width, acc=acc, final=(recv, lower_panel)
    )
    def halve(value, mask):
        size = value.shape[0] // 2
        bit = (row & mask) > 0
        low, high = value[:size], value[size:]
        return jnp.where(bit, high, low) + swap(jnp.where(bit, low, high), mask)

    def double(value, mask):
        bit = (row & mask) > 0
        got = swap(value, mask)
        return jnp.concatenate([jnp.where(bit, got, value), jnp.where(bit, value, got)])

    total = halve(halve(terms, CORE), X)
    total = total + swap(total, Z)
    total = total + swap(total, FAR)
    total = double(double(total, X), CORE)
    return panel, diag_inverse - total


def solution(mesh):
    n_row, n_col = mesh.shape["row"], mesh.shape["col"]

    def local(inverse_anc, lower_panel, structure, diag_inverse):
        rows, columns = inverse_anc.shape
        width = diag_inverse.shape[1]
        planned = (
            n_col == 2 and n_row == 2 * FAR and rows == 2 * width
            and structure.shape[0] == 1 and columns == FAR * rows
        )
        if planned:
            return local_two(n_row, inverse_anc, lower_panel, structure, diag_inverse)
        return local_any(inverse_anc, lower_panel, structure, diag_inverse)

    return jax.shard_map(
        local,
        mesh=mesh,
        in_specs=(P("row", "col"), P("row", "col"), P("col", None), P("col", None)),
        out_specs=(P("row", "col"), P("col", None)),
        check_vma=False,
    )
```

```python
import functools

import jax
import jax.numpy as jnp
from jax import lax
from jax.experimental import pallas as pl
from jax.experimental.pallas import tpu as pltpu
from jax.sharding import PartitionSpec as P


BOTH = ("row", "col")


def keep_rows(structure, first_row, row_count, sn_width):
    block_ids = (first_row + jnp.arange(row_count, dtype=jnp.int32)) // sn_width
    listed = jnp.any(structure[None, :, :] == block_ids[:, None, None], axis=2)
    return jnp.repeat(listed, sn_width, axis=1)


def local_any(inverse_anc, lower_panel, structure, diag_inverse):
    local_rows = inverse_anc.shape[0]
    sn_width = diag_inverse.shape[1]
    local_count = structure.shape[0]
    keep = keep_rows(structure, lax.axis_index("row") * local_rows, local_rows, sn_width)
    masked = jnp.where(keep, lower_panel, jnp.float32(0.0))
    rows = lax.all_gather(masked, "row", axis=0, tiled=True)
    rows = lax.all_to_all(rows, "col", split_axis=0, concat_axis=1, tiled=True)
    part = jnp.dot(inverse_anc, rows, precision=lax.Precision.HIGHEST)
    product = lax.psum_scatter(part, "col", scatter_dimension=1, tiled=True)
    panel = jnp.where(keep, -product, jnp.float32(0.0))
    terms = jnp.einsum(
        "ika,ikb->kab",
        masked.reshape(local_rows, local_count, sn_width),
        panel.reshape(local_rows, local_count, sn_width),
        precision=lax.Precision.HIGHEST,
    )
    total = lax.psum(terms.reshape(local_count * sn_width, sn_width), "row")
    return panel, diag_inverse - total


def split(value):
    high = value.astype(jnp.bfloat16)
    low = (value - high.astype(jnp.float32)).astype(jnp.bfloat16)
    return high, low


def dot3(a, b, dims):
    dot = lambda u, v: lax.dot_general(u, v, (dims, ((), ())), preferred_element_type=jnp.float32)
    return dot(a[0], b[0]) + (dot(a[0], b[1]) + dot(a[1], b[0]))


def product_kernel(slots, blocks, width, has_acc, final, table, *refs):
    count = len(slots)
    narrays = 1 + max(s[0] for s in slots)
    refs = list(refs)
    a_hbm = refs.pop(0)
    arrays = [refs.pop(0) for _ in range(narrays)]
    acc_in = refs.pop(0) if has_acc else None
    if final:
        recv, lower = refs.pop(0), refs.pop(0)
    out = refs.pop(0)
    if final:
        terms = refs.pop(0)
    a_buf, p_buf, a_sem, p_sem = refs
    row_on = [table[2 * count + rb] > 0 for rb in range(blocks)]

    def a_copy(p, rb):
        return pltpu.make_async_copy(
            a_hbm.at[pl.ds(rb * width, width), pl.ds(pl.multiple_of(table[p] * width, width), width)],
            a_buf.at[p, rb],
            a_sem.at[p, rb],
        )

    def p_copy(p):
        array, at = slots[p]
        return pltpu.make_async_copy(arrays[array].at[pl.ds(at * width, width), :], p_buf.at[p], p_sem.at[p])

    for p in range(count):
        @pl.when(table[count + p] > 0)
        def _(p=p):
            p_copy(p).start()
            for rb in range(blocks):
                @pl.when(row_on[rb])
                def _(rb=rb):
                    a_copy(p, rb).start()

    if has_acc:
        out[...] = acc_in[...]
    else:
        out[...] = jnp.zeros_like(out)
    for p in range(count):
        @pl.when(table[count + p] > 0)
        def _(p=p):
            p_copy(p).wait()
            piece = split(p_buf[p])
            for rb in range(blocks):
                @pl.when(row_on[rb])
                def _(rb=rb):
                    a_copy(p, rb).wait()
                    out[pl.ds(rb * width, width), :] += dot3(split(a_buf[p, rb]), piece, ((1,), (0,)))

    if final:
        terms[...] = jnp.zeros_like(terms)
        for rb in range(blocks):
            rows = pl.ds(rb * width, width)

            @pl.when(row_on[rb])
            def _(rows=rows):
                panel = -(out[rows, :] + recv[rows, :])
                out[rows, :] = panel
                terms[...] += dot3(split(lower[rows, :]), split(panel), ((0,), (0,)))

            @pl.when(jnp.logical_not(row_on[rb]))
            def _(rows=rows):
                out[rows, :] = jnp.zeros((width, out.shape[1]), jnp.float32)


def product(table, inverse_anc, arrays, slots, width, acc=None, final=None):
    rows = inverse_anc.shape[0]
    blocks = rows // width
    count = len(slots)
    any_spec = pl.BlockSpec(memory_space=pl.ANY)
    vmem = pl.BlockSpec(memory_space=pltpu.VMEM)
    operands = [inverse_anc, *arrays]
    specs = [any_spec] * len(operands)
    if acc is not None:
        operands.append(acc)
        specs.append(vmem)
    if final is not None:
        operands += list(final)
        specs += [vmem, vmem]
    shapes = [jax.ShapeDtypeStruct((rows, width), jnp.float32)]
    if final is not None:
        shapes.append(jax.ShapeDtypeStruct((width, width), jnp.float32))
    return pl.pallas_call(
        functools.partial(product_kernel, slots, blocks, width, acc is not None, final is not None),
        out_shape=shapes,
        grid_spec=pltpu.PrefetchScalarGridSpec(
            num_scalar_prefetch=1,
            grid=(1,),
            in_specs=specs,
            out_specs=[vmem] * len(shapes),
            scratch_shapes=[
                pltpu.VMEM((count, blocks, width, width), jnp.float32),
                pltpu.VMEM((count, width, width), jnp.float32),
                pltpu.SemaphoreType.DMA((count, blocks)),
                pltpu.SemaphoreType.DMA((count,)),
            ],
        ),
        compiler_params=pltpu.CompilerParams(vmem_limit_bytes=20 * 1024 * 1024),
        cost_estimate=pl.CostEstimate(
            flops=6 * rows * width * width * count // 4,
            bytes_accessed=4 * rows * width * count // 2,
            transcendentals=0,
        ),
    )(table, *operands)


CORE, X, Z, FAR = 1, 2, 4, 8
FIRST = ((0, 0), (0, 1), (X, 0), (Z, 1))
SECOND = ((Z, 0), (Z | X, 0), (X, 1), (Z | X, 1))


def with_sibling(order):
    return order + tuple((m ^ CORE, h) for m, h in order)


def local_two(n_row, inverse_anc, lower_panel, structure, diag_inverse):
    n_col = 2
    rows = inverse_anc.shape[0]
    width = diag_inverse.shape[1]
    row, col = lax.axis_index("row"), lax.axis_index("col")
    near = (row // FAR) == col
    flip = [(0, 1), (1, 0)]

    def swap(value, mask):
        return lax.ppermute(value, "row", [(i, i ^ mask) for i in range(n_row)])

    def linear(r, c):
        return r * n_col + c

    every = [(r, c) for r in range(n_row) for c in range(n_col)]
    first = [
        (linear(r, c), linear(r ^ FAR, c) if r // FAR == c else linear(r, 1 - c)) for r, c in every
    ]
    second = [(linear(r, c), linear(r ^ FAR, 1 - c)) for r, c in every if r // FAR != c]
    got_first = lax.ppermute(lower_panel, BOTH, first)
    got_second = lax.ppermute(lower_panel, BOTH, second)
    other_structure = lax.ppermute(structure, "col", flip)
    q_own = jnp.where(near, lower_panel, got_first)
    q_other = jnp.where(near, got_first, got_second)

    def table(listed, order):
        order = with_sibling(order)
        block = ((row % FAR) ^ jnp.array([m for m, _ in order], jnp.int32)) * 2
        block = block + jnp.array([h for _, h in order], jnp.int32)
        ids = jnp.concatenate([block + col * 2 * FAR, row * 2 + jnp.arange(2, dtype=jnp.int32)])
        on = jnp.any(ids[:, None] == listed[0][None, :], axis=1).astype(jnp.int32)
        return jnp.concatenate([block, on])

    half = rows // 2
    s0 = jnp.concatenate([q_other[:half], q_own[:half]])
    s1 = jnp.concatenate([q_other[half:], q_own[half:]])
    x1 = swap(s0, X)
    z1 = swap(s1, Z)
    got = []
    for at in (0, 1):
        part = slice(at * half, (at + 1) * half)
        z2 = swap(jnp.concatenate([s0[part], x1[part]]), Z)
        x2 = swap(jnp.concatenate([s1[part], z1[part]]), X)
        got.append([z2, x2])
    near_arrays = [s0, s1, x1, z1]
    near_arrays += [swap(v, CORE) for v in near_arrays]
    far_arrays = [v + [swap(u, CORE) for u in v] for v in got]

    def slots1(at):
        return tuple((i, at) for i in range(8))

    slots2 = tuple((i, h) for i in range(4) for h in range(2))
    (part,) = product(table(other_structure, FIRST), inverse_anc, near_arrays, slots1(0), width)
    (part,) = product(
        table(other_structure, SECOND), inverse_anc, far_arrays[0], slots2, width, acc=part
    )
    recv = lax.ppermute(part, "col", flip)
    (acc,) = product(table(structure, FIRST), inverse_anc, near_arrays, slots1(1), width)
    panel, terms = product(
        table(structure, SECOND), inverse_anc, far_arrays[1], slots2, width,
        acc=acc, final=(recv, lower_panel),
    )

    def halve(value, mask):
        size = value.shape[0] // 2
        bit = (row & mask) > 0
        low, high = value[:size], value[size:]
        return jnp.where(bit, high, low) + swap(jnp.where(bit, low, high), mask)

    def double(value, mask):
        bit = (row & mask) > 0
        got = swap(value, mask)
        return jnp.concatenate([jnp.where(bit, got, value), jnp.where(bit, value, got)])

    total = halve(halve(terms, CORE), X)
    total = total + swap(total, Z) + swap(total, FAR) + swap(total, FAR | Z)
    total = double(double(total, X), CORE)
    return panel, diag_inverse - total


def solution(mesh):
    n_row, n_col = mesh.shape["row"], mesh.shape["col"]

    def local(inverse_anc, lower_panel, structure, diag_inverse):
        rows, columns = inverse_anc.shape
        width = diag_inverse.shape[1]
        planned = (
            n_col == 2 and n_row == 2 * FAR and rows == 2 * width
            and structure.shape[0] == 1 and columns == FAR * rows
        )
        if planned:
            return local_two(n_row, inverse_anc, lower_panel, structure, diag_inverse)
        return local_any(inverse_anc, lower_panel, structure, diag_inverse)

    return jax.shard_map(
        local,
        mesh=mesh,
        in_specs=(P("row", "col"), P("row", "col"), P("col", None), P("col", None)),
        out_specs=(P("row", "col"), P("col", None)),
        check_vma=False,
    )
```

```python
import functools

import jax
import jax.numpy as jnp
from jax import lax
from jax.experimental import pallas as pl
from jax.experimental.pallas import tpu as pltpu
from jax.sharding import PartitionSpec as P


BOTH = ("row", "col")


def keep_rows(structure, first_row, row_count, sn_width):
    block_ids = (first_row + jnp.arange(row_count, dtype=jnp.int32)) // sn_width
    listed = jnp.any(structure[None, :, :] == block_ids[:, None, None], axis=2)
    return jnp.repeat(listed, sn_width, axis=1)


def local_any(inverse_anc, lower_panel, structure, diag_inverse):
    local_rows = inverse_anc.shape[0]
    sn_width = diag_inverse.shape[1]
    local_count = structure.shape[0]
    keep = keep_rows(structure, lax.axis_index("row") * local_rows, local_rows, sn_width)
    masked = jnp.where(keep, lower_panel, jnp.float32(0.0))
    rows = lax.all_gather(masked, "row", axis=0, tiled=True)
    rows = lax.all_to_all(rows, "col", split_axis=0, concat_axis=1, tiled=True)
    part = jnp.dot(inverse_anc, rows, precision=lax.Precision.HIGHEST)
    product = lax.psum_scatter(part, "col", scatter_dimension=1, tiled=True)
    panel = jnp.where(keep, -product, jnp.float32(0.0))
    terms = jnp.einsum(
        "ika,ikb->kab",
        masked.reshape(local_rows, local_count, sn_width),
        panel.reshape(local_rows, local_count, sn_width),
        precision=lax.Precision.HIGHEST,
    )
    total = lax.psum(terms.reshape(local_count * sn_width, sn_width), "row")
    return panel, diag_inverse - total


def split(value):
    high = value.astype(jnp.bfloat16)
    low = (value - high.astype(jnp.float32)).astype(jnp.bfloat16)
    return high, low


def dot3(a, b, dims):
    dot = lambda u, v: lax.dot_general(u, v, (dims, ((), ())), preferred_element_type=jnp.float32)
    return dot(a[0], b[0]) + (dot(a[0], b[1]) + dot(a[1], b[0]))


def product_kernel(slots, blocks, width, has_acc, final, table, *refs):
    count = len(slots)
    narrays = 1 + max(s[0] for s in slots)
    refs = list(refs)
    a_hbm = refs.pop(0)
    arrays = [refs.pop(0) for _ in range(narrays)]
    acc_in = refs.pop(0) if has_acc else None
    extra = refs.pop(0) if final else None
    out = refs.pop(0)
    terms = refs.pop(0) if final == "terms" else None
    a_buf, p_buf, a_sem, p_sem = refs
    row_on = [table[2 * count + rb] > 0 for rb in range(blocks)]

    def a_copy(p, rb):
        return pltpu.make_async_copy(
            a_hbm.at[pl.ds(rb * width, width), pl.ds(pl.multiple_of(table[p] * width, width), width)],
            a_buf.at[p, rb],
            a_sem.at[p, rb],
        )

    def p_copy(p):
        array, at = slots[p]
        return pltpu.make_async_copy(arrays[array].at[pl.ds(at * width, width), :], p_buf.at[p], p_sem.at[p])

    for p in range(count):
        @pl.when(table[count + p] > 0)
        def _(p=p):
            p_copy(p).start()
            for rb in range(blocks):
                @pl.when(row_on[rb])
                def _(rb=rb):
                    a_copy(p, rb).start()

    if has_acc:
        out[...] = acc_in[...]
    else:
        out[...] = jnp.zeros_like(out)
    for p in range(count):
        @pl.when(table[count + p] > 0)
        def _(p=p):
            p_copy(p).wait()
            piece = split(p_buf[p])
            for rb in range(blocks):
                @pl.when(row_on[rb])
                def _(rb=rb):
                    a_copy(p, rb).wait()
                    out[pl.ds(rb * width, width), :] += dot3(split(a_buf[p, rb]), piece, ((1,), (0,)))

    if final == "terms":
        terms[...] = jnp.zeros_like(terms)
        for rb in range(blocks):
            rows = pl.ds(rb * width, width)

            @pl.when(row_on[rb])
            def _(rows=rows):
                terms[...] += dot3(split(extra[rows, :]), split(out[rows, :]), ((0,), (0,)))

        @pl.when(table[2 * count + blocks] > 0)
        def _():
            terms[...] += terms[...].T

    if final == "panel":
        for rb in range(blocks):
            rows = pl.ds(rb * width, width)

            @pl.when(row_on[rb])
            def _(rows=rows):
                out[rows, :] = -(out[rows, :] + extra[rows, :])

            @pl.when(jnp.logical_not(row_on[rb]))
            def _(rows=rows):
                out[rows, :] = jnp.zeros((width, out.shape[1]), jnp.float32)


def product(table, inverse_anc, arrays, slots, width, acc=None, final=None, extra=None):
    rows = inverse_anc.shape[0]
    blocks = rows // width
    count = len(slots)
    any_spec = pl.BlockSpec(memory_space=pl.ANY)
    vmem = pl.BlockSpec(memory_space=pltpu.VMEM)
    operands = [pltpu.with_memory_space_constraint(inverse_anc, pltpu.HBM), *arrays]
    specs = [pl.BlockSpec(memory_space=pltpu.HBM)] + [any_spec] * len(arrays)
    for more in (acc, extra):
        if more is not None:
            operands.append(more)
            specs.append(vmem)
    shapes = [jax.ShapeDtypeStruct((rows, width), jnp.float32)]
    if final == "terms":
        shapes.append(jax.ShapeDtypeStruct((width, width), jnp.float32))
    return pl.pallas_call(
        functools.partial(product_kernel, slots, blocks, width, acc is not None, final),
        out_shape=shapes,
        grid_spec=pltpu.PrefetchScalarGridSpec(
            num_scalar_prefetch=1,
            grid=(1,),
            in_specs=specs,
            out_specs=[vmem] * len(shapes),
            scratch_shapes=[
                pltpu.VMEM((count, blocks, width, width), jnp.float32),
                pltpu.VMEM((count, width, width), jnp.float32),
                pltpu.SemaphoreType.DMA((count, blocks)),
                pltpu.SemaphoreType.DMA((count,)),
            ],
        ),
        compiler_params=pltpu.CompilerParams(vmem_limit_bytes=13 * 1024 * 1024),
        cost_estimate=pl.CostEstimate(
            flops=6 * rows * width * width * count // 4,
            bytes_accessed=4 * rows * width * count // 2,
            transcendentals=0,
        ),
    )(table, *operands)


CORE, X, Z, FAR = 1, 2, 4, 8
FIRST = ((0, 0), (0, 1), (X, 0), (Z, 1))
SECOND = ((Z, 0), (Z | X, 0), (X, 1), (Z | X, 1))
SLOTS1 = ((0, 0), (0, 1), (1, 0), (2, 0), (3, 0), (3, 1), (4, 0), (5, 0))
SLOTS2 = ((0, 0), (0, 1), (1, 0), (1, 1), (2, 0), (2, 1), (3, 0), (3, 1))


def local_two(n_row, inverse_anc, lower_panel, structure, diag_inverse):
    n_col = 2
    rows = inverse_anc.shape[0]
    width = diag_inverse.shape[1]
    half = rows // 2
    row, col = lax.axis_index("row"), lax.axis_index("col")
    near = (row // FAR) == col
    every = [(r, c) for r in range(n_row) for c in range(n_col)]

    def is_near(r, c):
        return r // FAR == c

    def move(value, mask, across, who=None):
        pairs = [
            (r * n_col + c, (r ^ mask) * n_col + (c ^ across))
            for r, c in every
            if who is None or is_near(r, c) == who
        ]
        return lax.ppermute(value, BOTH, pairs)

    def table(listed, order, who):
        order = order + tuple((m ^ CORE, h) for m, h in order)
        block = ((row % FAR) ^ jnp.array([m for m, _ in order], jnp.int32)) * 2
        block = block + jnp.array([h for _, h in order], jnp.int32)
        ids = jnp.concatenate([block + col * 2 * FAR, row * 2 + jnp.arange(2, dtype=jnp.int32)])
        on = jnp.any(ids[:, None] == listed[0][None, :], axis=1)
        count = len(order)
        if who is not None:
            on = on & ((jnp.arange(count + 2) >= count) | (near == who))
        far = jnp.logical_not(near) if who is None else jnp.zeros((), jnp.bool_)
        return jnp.concatenate([block, on.astype(jnp.int32), far.astype(jnp.int32)[None]])

    def step_one(q, who):
        return move(q[:half], X, 0, who), move(q[half:], Z, 0, who)

    def step_two(q, one, who):
        z2 = move(jnp.concatenate([q[:half], one[0]]), Z, 0, who)
        return z2, move(jnp.concatenate([q[half:], one[1]]), X, 0, who)

    def with_sibling(arrays, who):
        return list(arrays) + [move(v, CORE, 0, who) for v in arrays]

    got_far = move(lower_panel, FAR, 1, False)
    lower_other = move(lower_panel, 0, 1)
    q_far = move(lower_panel, FAR, 0, True)
    other_structure = move(structure, 0, 1)

    n_one = step_one(lower_panel, True)
    n_two = step_two(lower_panel, n_one, True)
    n_first = with_sibling([lower_panel, *n_one], True)
    n_second = with_sibling(n_two, True)
    q_other = jnp.where(near, lower_other, got_far)
    o_one = step_one(q_other, None)
    o_two = step_two(q_other, o_one, None)
    o_first = with_sibling([q_other, *o_one], None)
    o_second = with_sibling(o_two, None)
    f_one = step_one(q_far, False)
    f_two = step_two(q_far, f_one, False)
    f_first = with_sibling([q_far, *f_one], False)
    f_second = with_sibling(f_two, False)

    (own,) = product(table(structure, FIRST, True), inverse_anc, n_first, SLOTS1, width)
    own, own_terms = product(
        table(structure, SECOND, True), inverse_anc, n_second, SLOTS2, width,
        acc=own, final="terms", extra=lower_panel,
    )
    (part,) = product(table(other_structure, FIRST, None), inverse_anc, o_first, SLOTS1, width)
    part, other_terms = product(
        table(other_structure, SECOND, None), inverse_anc, o_second, SLOTS2, width,
        acc=part, final="terms", extra=lower_other,
    )
    recv = move(part, 0, 1)
    (own,) = product(table(structure, FIRST, False), inverse_anc, f_first, SLOTS1, width, acc=own)
    (panel,) = product(
        table(structure, SECOND, False), inverse_anc, f_second, SLOTS2, width,
        acc=own, final="panel", extra=recv,
    )

    def parts(value, mask):
        size = value.shape[0] // 2
        bit = (row & mask) > 0
        low, high = value[:size], value[size:]
        return jnp.where(bit, high, low), jnp.where(bit, low, high)

    def double(value, mask):
        bit = (row & mask) > 0
        got = move(value, mask, 0)
        return jnp.concatenate([jnp.where(bit, got, value), jnp.where(bit, value, got)])

    u_keep, u_send = parts(own_terms, CORE)
    v_keep, v_send = parts(other_terms, CORE)
    size = u_keep.shape[0]
    got = move(jnp.concatenate([u_send, v_send]), CORE, 0)
    u_keep, u_send = parts(u_keep + got[:size], X)
    v_keep, v_send = parts(v_keep + got[size:], X)
    total = u_keep + move(u_send, X, 0) + move(v_keep, 0, 1) + move(v_send, X, 1)
    total = total + move(total, Z, 0) + move(total, FAR, 0) + move(total, FAR | Z, 0)
    total = double(double(total, X), CORE)
    return panel, diag_inverse + total


def solution(mesh):
    n_row, n_col = mesh.shape["row"], mesh.shape["col"]

    def local(inverse_anc, lower_panel, structure, diag_inverse):
        rows, columns = inverse_anc.shape
        width = diag_inverse.shape[1]
        planned = (
            n_col == 2 and n_row == 2 * FAR and rows == 2 * width
            and structure.shape[0] == 1 and columns == FAR * rows
        )
        if planned:
            return local_two(n_row, inverse_anc, lower_panel, structure, diag_inverse)
        return local_any(inverse_anc, lower_panel, structure, diag_inverse)

    return jax.shard_map(
        local,
        mesh=mesh,
        in_specs=(P("row", "col"), P("row", "col"), P("col", None), P("col", None)),
        out_specs=(P("row", "col"), P("col", None)),
        check_vma=False,
    )
```

```python
import functools

import jax
import jax.numpy as jnp
from jax import lax
from jax.experimental import pallas as pl
from jax.experimental.pallas import tpu as pltpu
from jax.sharding import PartitionSpec as P


BOTH = ("row", "col")


def keep_rows(structure, first_row, row_count, sn_width):
    block_ids = (first_row + jnp.arange(row_count, dtype=jnp.int32)) // sn_width
    listed = jnp.any(structure[None, :, :] == block_ids[:, None, None], axis=2)
    return jnp.repeat(listed, sn_width, axis=1)


def local_any(inverse_anc, lower_panel, structure, diag_inverse):
    local_rows = inverse_anc.shape[0]
    sn_width = diag_inverse.shape[1]
    local_count = structure.shape[0]
    keep = keep_rows(structure, lax.axis_index("row") * local_rows, local_rows, sn_width)
    masked = jnp.where(keep, lower_panel, jnp.float32(0.0))
    rows = lax.all_gather(masked, "row", axis=0, tiled=True)
    rows = lax.all_to_all(rows, "col", split_axis=0, concat_axis=1, tiled=True)
    part = jnp.dot(inverse_anc, rows, precision=lax.Precision.HIGHEST)
    product = lax.psum_scatter(part, "col", scatter_dimension=1, tiled=True)
    panel = jnp.where(keep, -product, jnp.float32(0.0))
    terms = jnp.einsum(
        "ika,ikb->kab",
        masked.reshape(local_rows, local_count, sn_width),
        panel.reshape(local_rows, local_count, sn_width),
        precision=lax.Precision.HIGHEST,
    )
    total = lax.psum(terms.reshape(local_count * sn_width, sn_width), "row")
    return panel, diag_inverse - total


def split(value):
    high = value.astype(jnp.bfloat16)
    low = (value - high.astype(jnp.float32)).astype(jnp.bfloat16)
    return high, low


def dot3(a, b, dims):
    dot = lambda u, v: lax.dot_general(u, v, (dims, ((), ())), preferred_element_type=jnp.float32)
    return dot(a[0], b[0]) + (dot(a[0], b[1]) + dot(a[1], b[0]))


def product_kernel(slots, blocks, width, has_acc, final, table, *refs):
    count = len(slots)
    narrays = 1 + max(s[0] for s in slots)
    refs = list(refs)
    a_hbm = refs.pop(0)
    arrays = [refs.pop(0) for _ in range(narrays)]
    acc_in = refs.pop(0) if has_acc else None
    extra_in = refs.pop(0) if final else None
    out = refs.pop(0)
    terms = refs.pop(0) if final == "terms" else None
    a_buf, p_buf, extra, a_sem, p_sem, one_sem = refs
    row_on = [table[2 * count + rb] > 0 for rb in range(blocks)]

    def a_copy(p, rb):
        return pltpu.make_async_copy(
            a_hbm.at[pl.ds(rb * width, width), pl.ds(pl.multiple_of(table[p] * width, width), width)],
            a_buf.at[p, rb],
            a_sem.at[p, rb],
        )

    def p_copy(p):
        array, at = slots[p]
        return pltpu.make_async_copy(arrays[array].at[pl.ds(at * width, width), :], p_buf.at[p], p_sem.at[p])

    if has_acc:
        acc_copy = pltpu.make_async_copy(acc_in, out, one_sem.at[0])
        acc_copy.start()
    for p in range(count):
        @pl.when(table[count + p] > 0)
        def _(p=p):
            p_copy(p).start()
            for rb in range(blocks):
                @pl.when(row_on[rb])
                def _(rb=rb):
                    a_copy(p, rb).start()

    if final:
        extra_copy = pltpu.make_async_copy(extra_in, extra, one_sem.at[1])
        extra_copy.start()
    if has_acc:
        acc_copy.wait()
    else:
        out[...] = jnp.zeros_like(out)
    for p in range(count):
        @pl.when(table[count + p] > 0)
        def _(p=p):
            p_copy(p).wait()
            piece = split(p_buf[p])
            for rb in range(blocks):
                @pl.when(row_on[rb])
                def _(rb=rb):
                    a_copy(p, rb).wait()
                    out[pl.ds(rb * width, width), :] += dot3(split(a_buf[p, rb]), piece, ((1,), (0,)))

    if final:
        extra_copy.wait()
    if final == "terms":
        terms[...] = jnp.zeros_like(terms)
        for rb in range(blocks):
            rows = pl.ds(rb * width, width)

            @pl.when(row_on[rb])
            def _(rows=rows):
                terms[...] += dot3(split(extra[rows, :]), split(out[rows, :]), ((0,), (0,)))

        @pl.when(table[2 * count + blocks] > 0)
        def _():
            terms[...] += terms[...].T

    if final == "panel":
        for rb in range(blocks):
            rows = pl.ds(rb * width, width)

            @pl.when(row_on[rb])
            def _(rows=rows):
                out[rows, :] = -(out[rows, :] + extra[rows, :])

            @pl.when(jnp.logical_not(row_on[rb]))
            def _(rows=rows):
                out[rows, :] = jnp.zeros((width, out.shape[1]), jnp.float32)


def product(table, inverse_anc, arrays, slots, width, acc=None, final=None, extra=None):
    rows = inverse_anc.shape[0]
    blocks = rows // width
    count = len(slots)
    any_spec = pl.BlockSpec(memory_space=pl.ANY)
    vmem = pl.BlockSpec(memory_space=pltpu.VMEM)
    operands = [pltpu.with_memory_space_constraint(inverse_anc, pltpu.HBM), *arrays]
    specs = [pl.BlockSpec(memory_space=pltpu.HBM)] + [any_spec] * len(arrays)
    for more in (acc, extra):
        if more is not None:
            operands.append(more)
            specs.append(any_spec)
    shapes = [jax.ShapeDtypeStruct((rows, width), jnp.float32)]
    if final == "terms":
        shapes.append(jax.ShapeDtypeStruct((width, width), jnp.float32))
    return pl.pallas_call(
        functools.partial(product_kernel, slots, blocks, width, acc is not None, final),
        out_shape=shapes,
        grid_spec=pltpu.PrefetchScalarGridSpec(
            num_scalar_prefetch=1,
            grid=(1,),
            in_specs=specs,
            out_specs=[vmem] * len(shapes),
            scratch_shapes=[
                pltpu.VMEM((count, blocks, width, width), jnp.float32),
                pltpu.VMEM((count, width, width), jnp.float32),
                pltpu.VMEM((rows, width), jnp.float32),
                pltpu.SemaphoreType.DMA((count, blocks)),
                pltpu.SemaphoreType.DMA((count,)),
                pltpu.SemaphoreType.DMA((2,)),
            ],
        ),
        compiler_params=pltpu.CompilerParams(vmem_limit_bytes=13 * 1024 * 1024),
        cost_estimate=pl.CostEstimate(
            flops=6 * rows * width * width * count // 4,
            bytes_accessed=4 * rows * width * count // 2,
            transcendentals=0,
        ),
    )(table, *operands)


CORE, X, Z, FAR = 1, 2, 4, 8
FIRST = ((0, 0), (0, 1), (X, 0), (Z, 1))
SECOND = ((Z, 0), (Z | X, 0), (X, 1), (Z | X, 1))
SLOTS1 = ((0, 0), (0, 1), (1, 0), (2, 0), (3, 0), (3, 1), (4, 0), (5, 0))
SLOTS2 = ((0, 0), (0, 1), (1, 0), (1, 1), (2, 0), (2, 1), (3, 0), (3, 1))


def local_two(n_row, inverse_anc, lower_panel, structure, diag_inverse):
    n_col = 2
    rows = inverse_anc.shape[0]
    width = diag_inverse.shape[1]
    half = rows // 2
    row, col = lax.axis_index("row"), lax.axis_index("col")
    near = (row // FAR) == col
    every = [(r, c) for r in range(n_row) for c in range(n_col)]

    def is_near(r, c):
        return r // FAR == c

    def move(value, mask, across, who=None):
        pairs = [
            (r * n_col + c, (r ^ mask) * n_col + (c ^ across))
            for r, c in every
            if who is None or is_near(r, c) == who
        ]
        return lax.ppermute(value, BOTH, pairs)

    def table(listed, order, who):
        order = order + tuple((m ^ CORE, h) for m, h in order)
        block = ((row % FAR) ^ jnp.array([m for m, _ in order], jnp.int32)) * 2
        block = block + jnp.array([h for _, h in order], jnp.int32)
        ids = jnp.concatenate([block + col * 2 * FAR, row * 2 + jnp.arange(2, dtype=jnp.int32)])
        on = jnp.any(ids[:, None] == listed[0][None, :], axis=1)
        count = len(order)
        if who is not None:
            on = on & ((jnp.arange(count + 2) >= count) | (near == who))
        far = jnp.logical_not(near) if who is None else jnp.zeros((), jnp.bool_)
        return jnp.concatenate([block, on.astype(jnp.int32), far.astype(jnp.int32)[None]])

    def step_one(q, who):
        return move(q[:half], X, 0, who), move(q[half:], Z, 0, who)

    def step_two(q, one, who):
        first, second = jnp.concatenate([q[:half], one[0]]), jnp.concatenate([q[half:], one[1]])
        return move(first, Z, 0, who), move(second, X, 0, who)

    def with_sibling(arrays, who):
        return list(arrays) + [move(v, CORE, 0, who) for v in arrays]

    other_structure = move(structure, 0, 1)
    got_far = move(lower_panel, FAR, 1, False)
    lower_other = move(lower_panel, 0, 1)
    q_far = move(lower_panel, FAR, 0, True)

    n_one = step_one(lower_panel, True)
    n_two = step_two(lower_panel, n_one, True)
    n_first = with_sibling([lower_panel, *n_one], None)
    n_second = with_sibling(n_two, None)
    q_other = jnp.where(near, lower_other, got_far)
    o_one = step_one(q_other, None)
    o_two = step_two(q_other, o_one, None)
    o_first = with_sibling([q_other, *o_one], None)
    o_second = with_sibling(o_two, None)
    f_one = step_one(q_far, False)
    f_two = step_two(q_far, f_one, False)
    f_first = with_sibling([q_far, *f_one], None)
    f_second = with_sibling(f_two, None)

    (own,) = product(table(structure, FIRST, True), inverse_anc, n_first, SLOTS1, width)
    own, own_terms = product(
        table(structure, SECOND, True), inverse_anc, n_second, SLOTS2, width,
        acc=own, final="terms", extra=lower_panel,
    )
    (part,) = product(table(other_structure, FIRST, None), inverse_anc, o_first, SLOTS1, width)
    part, other_terms = product(
        table(other_structure, SECOND, None), inverse_anc, o_second, SLOTS2, width,
        acc=part, final="terms", extra=lower_other,
    )
    recv = move(part, 0, 1)
    (own,) = product(table(structure, FIRST, False), inverse_anc, f_first, SLOTS1, width, acc=own)
    (panel,) = product(
        table(structure, SECOND, False), inverse_anc, f_second, SLOTS2, width,
        acc=own, final="panel", extra=recv,
    )

    def parts(value, mask):
        size = value.shape[0] // 2
        bit = (row & mask) > 0
        low, high = value[:size], value[size:]
        return jnp.where(bit, high, low), jnp.where(bit, low, high)

    def double(value, mask):
        bit = (row & mask) > 0
        got = move(value, mask, 0)
        return jnp.concatenate([jnp.where(bit, got, value), jnp.where(bit, value, got)])

    u_keep, u_send = parts(own_terms, CORE)
    v_keep, v_send = parts(other_terms, CORE)
    size = u_keep.shape[0]
    got = move(jnp.concatenate([u_send, v_send]), CORE, 0)
    u_keep, u_send = parts(u_keep + got[:size], X)
    v_keep, v_send = parts(v_keep + got[size:], X)
    total = u_keep + move(u_send, X, 0) + move(v_keep, 0, 1) + move(v_send, X, 1)
    total = total + move(total, Z, 0) + move(total, FAR, 0) + move(total, FAR | Z, 0)
    total = double(double(total, X), CORE)
    return panel, diag_inverse + total


def solution(mesh):
    n_row, n_col = mesh.shape["row"], mesh.shape["col"]

    def local(inverse_anc, lower_panel, structure, diag_inverse):
        rows, columns = inverse_anc.shape
        width = diag_inverse.shape[1]
        planned = (
            n_col == 2 and n_row == 2 * FAR and rows == 2 * width
            and structure.shape[0] == 1 and columns == FAR * rows
        )
        if planned:
            return local_two(n_row, inverse_anc, lower_panel, structure, diag_inverse)
        return local_any(inverse_anc, lower_panel, structure, diag_inverse)

    return jax.shard_map(
        local,
        mesh=mesh,
        in_specs=(P("row", "col"), P("row", "col"), P("col", None), P("col", None)),
        out_specs=(P("row", "col"), P("col", None)),
        check_vma=False,
    )
```

```python
import functools

import jax
import jax.numpy as jnp
from jax import lax
from jax.experimental import pallas as pl
from jax.experimental.pallas import tpu as pltpu
from jax.sharding import PartitionSpec as P


BOTH = ("row", "col")


def keep_rows(structure, first_row, row_count, sn_width):
    block_ids = (first_row + jnp.arange(row_count, dtype=jnp.int32)) // sn_width
    listed = jnp.any(structure[None, :, :] == block_ids[:, None, None], axis=2)
    return jnp.repeat(listed, sn_width, axis=1)


def local_any(inverse_anc, lower_panel, structure, diag_inverse):
    local_rows = inverse_anc.shape[0]
    sn_width = diag_inverse.shape[1]
    local_count = structure.shape[0]
    keep = keep_rows(structure, lax.axis_index("row") * local_rows, local_rows, sn_width)
    masked = jnp.where(keep, lower_panel, jnp.float32(0.0))
    rows = lax.all_gather(masked, "row", axis=0, tiled=True)
    rows = lax.all_to_all(rows, "col", split_axis=0, concat_axis=1, tiled=True)
    part = jnp.dot(inverse_anc, rows, precision=lax.Precision.HIGHEST)
    product = lax.psum_scatter(part, "col", scatter_dimension=1, tiled=True)
    panel = jnp.where(keep, -product, jnp.float32(0.0))
    terms = jnp.einsum(
        "ika,ikb->kab",
        masked.reshape(local_rows, local_count, sn_width),
        panel.reshape(local_rows, local_count, sn_width),
        precision=lax.Precision.HIGHEST,
    )
    total = lax.psum(terms.reshape(local_count * sn_width, sn_width), "row")
    return panel, diag_inverse - total


def split(value):
    high = value.astype(jnp.bfloat16)
    low = (value - high.astype(jnp.float32)).astype(jnp.bfloat16)
    return high, low


def dot3(a, b, dims):
    dot = lambda u, v: lax.dot_general(u, v, (dims, ((), ())), preferred_element_type=jnp.float32)
    return dot(a[0], b[0]) + (dot(a[0], b[1]) + dot(a[1], b[0]))


def product_kernel(slots, blocks, width, has_acc, final, table, *refs):
    count = len(slots)
    narrays = 1 + max(s[0] for s in slots)
    refs = list(refs)
    a_hbm = refs.pop(0)
    arrays = [refs.pop(0) for _ in range(narrays)]
    acc_in = refs.pop(0) if has_acc else None
    extra_in = refs.pop(0) if final else None
    out = refs.pop(0)
    terms = refs.pop(0) if final else None
    a_buf, p_buf, extra, a_sem, p_sem, one_sem = refs
    row_on = [table[2 * count + rb] > 0 for rb in range(blocks)]
    all_on = functools.reduce(jnp.logical_and, row_on)
    dot = functools.partial(jnp.dot, preferred_element_type=jnp.float32)

    def a_copy(p, rb):
        return pltpu.make_async_copy(
            a_hbm.at[pl.ds(rb * width, width), pl.ds(pl.multiple_of(table[p] * width, width), width)],
            a_buf.at[p, rb],
            a_sem.at[p, rb],
        )

    def p_copy(p):
        array, at = slots[p]
        return pltpu.make_async_copy(arrays[array].at[pl.ds(at * width, width), :], p_buf.at[p], p_sem.at[p])

    if has_acc:
        acc_copy = pltpu.make_async_copy(acc_in, out, one_sem.at[0])
        acc_copy.start()
    for p in range(count):
        @pl.when(table[count + p] > 0)
        def _(p=p):
            p_copy(p).start()
            for rb in range(blocks):
                @pl.when(row_on[rb])
                def _(rb=rb):
                    a_copy(p, rb).start()

    if final:
        extra_copy = pltpu.make_async_copy(extra_in, extra, one_sem.at[1])
        extra_copy.start()
    if has_acc:
        acc_copy.wait()
    else:
        out[...] = jnp.zeros_like(out)

    def step(p, carry):
        @pl.when(table[count + p] > 0)
        def _():
            pltpu.make_async_copy(p_buf.at[p], p_buf.at[p], p_sem.at[p]).wait()
            high, low = split(p_buf[p])

            def add(first, size):
                for rb in range(first, first + size):
                    a_copy(p, rb).wait()
                a_high, a_low = split(a_buf[p, first : first + size].reshape(size * width, width))
                both = dot(jnp.concatenate([a_high, a_low]), high)
                total = both[: size * width] + (both[size * width :] + dot(a_high, low))
                out[pl.ds(first * width, size * width), :] += total

            @pl.when(all_on)
            def _():
                add(0, blocks)

            for rb in range(blocks):
                @pl.when(jnp.logical_not(all_on) & row_on[rb])
                def _(rb=rb):
                    add(rb, 1)

        return carry

    lax.fori_loop(0, count, step, 0)
    if final:
        extra_copy.wait()
        terms[...] = jnp.zeros_like(terms)
        for rb in range(blocks):
            rows = pl.ds(rb * width, width)

            @pl.when(row_on[rb])
            def _(rows=rows):
                terms[...] += dot3(split(extra[rows, :]), split(out[rows, :]), ((0,), (0,)))

        @pl.when(table[2 * count + blocks] > 0)
        def _():
            terms[...] += terms[...].T


def product(table, inverse_anc, arrays, slots, width, acc=None, extra=None):
    rows = inverse_anc.shape[0]
    blocks = rows // width
    count = len(slots)
    any_spec = pl.BlockSpec(memory_space=pl.ANY)
    vmem = pl.BlockSpec(memory_space=pltpu.VMEM)
    operands = [pltpu.with_memory_space_constraint(inverse_anc, pltpu.HBM), *arrays]
    specs = [pl.BlockSpec(memory_space=pltpu.HBM)] + [any_spec] * len(arrays)
    for more in (acc, extra):
        if more is not None:
            operands.append(more)
            specs.append(any_spec)
    shapes = [pltpu.HBM((rows, width), jnp.float32)]
    if extra is not None:
        shapes.append(jax.ShapeDtypeStruct((width, width), jnp.float32))
    return pl.pallas_call(
        functools.partial(product_kernel, slots, blocks, width, acc is not None, extra is not None),
        out_shape=shapes,
        grid_spec=pltpu.PrefetchScalarGridSpec(
            num_scalar_prefetch=1,
            grid=(1,),
            in_specs=specs,
            out_specs=[vmem] * len(shapes),
            scratch_shapes=[
                pltpu.VMEM((count, blocks, width, width), jnp.float32),
                pltpu.VMEM((count, width, width), jnp.float32),
                pltpu.VMEM((rows, width), jnp.float32),
                pltpu.SemaphoreType.DMA((count, blocks)),
                pltpu.SemaphoreType.DMA((count,)),
                pltpu.SemaphoreType.DMA((2,)),
            ],
        ),
        compiler_params=pltpu.CompilerParams(vmem_limit_bytes=20 * 1024 * 1024),
        cost_estimate=pl.CostEstimate(
            flops=6 * rows * width * width * count // 4,
            bytes_accessed=4 * rows * width * count // 2,
            transcendentals=0,
        ),
    )(table, *operands)


CORE, X, Z, FAR = 1, 2, 4, 8
FIRST = ((0, 0), (0, 1), (X, 0), (Z, 1), (1, 0), (1, 1), (X | 1, 0), (Z | 1, 1))
SECOND = tuple((m | c, h) for c in (0, 1) for m, h in ((Z, 0), (Z | X, 0), (X, 1), (Z | X, 1)))
WHOLE = tuple((m | c, h) for c in (0, 1) for m in (0, X, Z, Z | X) for h in (0, 1))
SLOTS1 = ((0, 0), (0, 1), (1, 0), (2, 0), (3, 0), (3, 1), (4, 0), (5, 0))
SLOTS2 = ((0, 0), (0, 1), (1, 0), (1, 1), (2, 0), (2, 1), (3, 0), (3, 1))
SLOTSW = tuple((i, h) for i in range(8) for h in (0, 1))
SLOTS12 = SLOTS1 + tuple((6 + i, h) for i, h in SLOTS2)


def local_two(n_row, inverse_anc, lower_panel, structure, diag_inverse):
    n_col = 2
    rows = inverse_anc.shape[0]
    width = diag_inverse.shape[1]
    half = rows // 2
    row, col = lax.axis_index("row"), lax.axis_index("col")
    near = (row // FAR) == col
    every = [(r, c) for r in range(n_row) for c in range(n_col)]

    def is_near(r, c):
        return r // FAR == c

    def move(value, mask, across, who=None):
        pairs = [
            (r * n_col + c, (r ^ mask) * n_col + (c ^ across))
            for r, c in every
            if who is None or is_near(r, c) == who
        ]
        return lax.ppermute(value, BOTH, pairs)

    def table(listed, order, who):
        block = ((row % FAR) ^ jnp.array([m for m, _ in order], jnp.int32)) * 2
        block = block + jnp.array([h for _, h in order], jnp.int32)
        ids = jnp.concatenate([block + col * 2 * FAR, row * 2 + jnp.arange(2, dtype=jnp.int32)])
        on = jnp.any(ids[:, None] == listed[0][None, :], axis=1)
        count = len(order)
        if who is not None:
            on = on & ((jnp.arange(count + 2) >= count) | (near == who))
        far = jnp.logical_not(near) if who is None else jnp.zeros((), jnp.bool_)
        return jnp.concatenate([block, on.astype(jnp.int32), far.astype(jnp.int32)[None]])

    def step_one(q, who):
        return move(q[:half], X, 0, who), move(q[half:], Z, 0, who)

    def step_two(q, one, who):
        first, second = jnp.concatenate([q[:half], one[0]]), jnp.concatenate([q[half:], one[1]])
        return move(first, Z, 0, who), move(second, X, 0, who)

    def with_sibling(arrays, who):
        return list(arrays) + [move(v, CORE, 0, who) for v in arrays]

    other_structure = move(structure, 0, 1)
    got_far = move(lower_panel, FAR, 1, False)
    lower_other = move(lower_panel, 0, 1)
    n_z = move(lower_panel, Z, 0, True)
    n_x = move(lower_panel, X, 0, True)
    q_far = move(lower_panel, FAR, 0, True)
    n_zx = move(n_z, X, 0, True)
    n_all = with_sibling([lower_panel, n_x, n_z, n_zx], None)
    in_hbm = lambda v: pltpu.with_memory_space_constraint(v, pltpu.HBM)
    n_all[0] = in_hbm(lower_panel)
    q_other = jnp.where(near, lower_other, got_far)
    o_one = step_one(q_other, None)
    o_two = step_two(q_other, o_one, None)
    o_first = with_sibling([q_other, *o_one], None)
    o_second = with_sibling(o_two, None)
    f_one = step_one(q_far, False)
    f_two = step_two(q_far, f_one, False)
    f_first = with_sibling([q_far, *f_one], None)
    f_second = with_sibling(f_two, None)

    own, own_terms = product(
        table(structure, WHOLE, True), inverse_anc, n_all, SLOTSW, width, extra=n_all[0]
    )
    (part,) = product(table(other_structure, FIRST, None), inverse_anc, o_first, SLOTS1, width)
    part, other_terms = product(
        table(other_structure, SECOND, None), inverse_anc, o_second, SLOTS2, width,
        acc=in_hbm(part), extra=lower_other,
    )
    recv = move(part, 0, 1)
    (own,) = product(
        table(structure, FIRST + SECOND, False), inverse_anc, f_first + f_second, SLOTS12, width,
        acc=in_hbm(own),
    )
    keep = keep_rows(structure, row * rows, rows, width)
    panel = jnp.where(keep, -(own + recv), jnp.float32(0.0))

    def parts(value, mask):
        size = value.shape[0] // 2
        bit = (row & mask) > 0
        low, high = value[:size], value[size:]
        return jnp.where(bit, high, low), jnp.where(bit, low, high)

    def double(value, mask):
        bit = (row & mask) > 0
        got = move(value, mask, 0)
        return jnp.concatenate([jnp.where(bit, got, value), jnp.where(bit, value, got)])

    u_keep, u_send = parts(own_terms, CORE)
    v_keep, v_send = parts(other_terms, CORE)
    size = u_keep.shape[0]
    got = move(jnp.concatenate([u_send, v_send]), CORE, 0)
    u_keep, u_send = parts(u_keep + got[:size], X)
    v_keep, v_send = parts(v_keep + got[size:], X)
    total = u_keep + move(u_send, X, 0) + move(v_keep, 0, 1) + move(v_send, X, 1)
    total = total + move(total, Z, 0) + move(total, FAR, 0) + move(total, FAR | Z, 0)
    total = double(double(total, X), CORE)
    return panel, diag_inverse + total


def solution(mesh):
    n_row, n_col = mesh.shape["row"], mesh.shape["col"]

    def local(inverse_anc, lower_panel, structure, diag_inverse):
        rows, columns = inverse_anc.shape
        width = diag_inverse.shape[1]
        planned = (
            n_col == 2 and n_row == 2 * FAR and rows == 2 * width
            and structure.shape[0] == 1 and columns == FAR * rows
        )
        if planned:
            return local_two(n_row, inverse_anc, lower_panel, structure, diag_inverse)
        return local_any(inverse_anc, lower_panel, structure, diag_inverse)

    return jax.shard_map(
        local,
        mesh=mesh,
        in_specs=(P("row", "col"), P("row", "col"), P("col", None), P("col", None)),
        out_specs=(P("row", "col"), P("col", None)),
        check_vma=False,
    )
```

```python
import functools

import jax
import jax.numpy as jnp
from jax import lax
from jax.experimental import pallas as pl
from jax.experimental.pallas import tpu as pltpu
from jax.sharding import PartitionSpec as P


BOTH = ("row", "col")


def keep_rows(structure, first_row, row_count, sn_width):
    block_ids = (first_row + jnp.arange(row_count, dtype=jnp.int32)) // sn_width
    listed = jnp.any(structure[None, :, :] == block_ids[:, None, None], axis=2)
    return jnp.repeat(listed, sn_width, axis=1)


def local_any(inverse_anc, lower_panel, structure, diag_inverse):
    local_rows = inverse_anc.shape[0]
    sn_width = diag_inverse.shape[1]
    local_count = structure.shape[0]
    keep = keep_rows(structure, lax.axis_index("row") * local_rows, local_rows, sn_width)
    masked = jnp.where(keep, lower_panel, jnp.float32(0.0))
    rows = lax.all_gather(masked, "row", axis=0, tiled=True)
    rows = lax.all_to_all(rows, "col", split_axis=0, concat_axis=1, tiled=True)
    part = jnp.dot(inverse_anc, rows, precision=lax.Precision.HIGHEST)
    product = lax.psum_scatter(part, "col", scatter_dimension=1, tiled=True)
    panel = jnp.where(keep, -product, jnp.float32(0.0))
    terms = jnp.einsum(
        "ika,ikb->kab",
        masked.reshape(local_rows, local_count, sn_width),
        panel.reshape(local_rows, local_count, sn_width),
        precision=lax.Precision.HIGHEST,
    )
    total = lax.psum(terms.reshape(local_count * sn_width, sn_width), "row")
    return panel, diag_inverse - total


def split(value):
    high = value.astype(jnp.bfloat16)
    low = (value - high.astype(jnp.float32)).astype(jnp.bfloat16)
    return high, low


def dot3(a, b, dims):
    dot = lambda u, v: lax.dot_general(u, v, (dims, ((), ())), preferred_element_type=jnp.float32)
    return dot(a[0], b[0]) + (dot(a[0], b[1]) + dot(a[1], b[0]))


def product_kernel(slots, blocks, width, has_acc, final, table, *refs):
    count = len(slots)
    narrays = 1 + max(s[0] for s in slots)
    refs = list(refs)
    a_hbm = refs.pop(0)
    arrays = [refs.pop(0) for _ in range(narrays)]
    acc_in = refs.pop(0) if has_acc else None
    extra_in = refs.pop(0) if final else None
    out = refs.pop(0)
    terms = refs.pop(0) if final else None
    a_buf, p_buf, extra, a_sem, p_sem, one_sem = refs
    row_on = [table[2 * count + rb] > 0 for rb in range(blocks)]
    all_on = functools.reduce(jnp.logical_and, row_on)
    dot = functools.partial(jnp.dot, preferred_element_type=jnp.float32)

    def a_copy(p, rb):
        return pltpu.make_async_copy(
            a_hbm.at[pl.ds(rb * width, width), pl.ds(pl.multiple_of(table[p] * width, width), width)],
            a_buf.at[p, rb],
            a_sem.at[p, rb],
        )

    def p_copy(p):
        array, at = slots[p]
        return pltpu.make_async_copy(arrays[array].at[pl.ds(at * width, width), :], p_buf.at[p], p_sem.at[p])

    if has_acc:
        acc_copy = pltpu.make_async_copy(acc_in, out, one_sem.at[0])
        acc_copy.start()
    for p in range(count):
        @pl.when(table[count + p] > 0)
        def _(p=p):
            p_copy(p).start()
            for rb in range(blocks):
                @pl.when(row_on[rb])
                def _(rb=rb):
                    a_copy(p, rb).start()

    if final:
        extra_copy = pltpu.make_async_copy(extra_in, extra, one_sem.at[1])
        extra_copy.start()
    if has_acc:
        acc_copy.wait()
    else:
        out[...] = jnp.zeros_like(out)

    def step(p, carry):
        @pl.when(table[count + p] > 0)
        def _():
            pltpu.make_async_copy(p_buf.at[p], p_buf.at[p], p_sem.at[p]).wait()
            high, low = split(p_buf[p])

            def add(first, size):
                for rb in range(first, first + size):
                    a_copy(p, rb).wait()
                a_high, a_low = split(a_buf[p, first : first + size].reshape(size * width, width))
                both = dot(jnp.concatenate([a_high, a_low]), high)
                total = both[: size * width] + (both[size * width :] + dot(a_high, low))
                out[pl.ds(first * width, size * width), :] += total

            @pl.when(all_on)
            def _():
                add(0, blocks)

            for rb in range(blocks):
                @pl.when(jnp.logical_not(all_on) & row_on[rb])
                def _(rb=rb):
                    add(rb, 1)

        return carry

    lax.fori_loop(0, count, step, 0)
    if final:
        extra_copy.wait()
        terms[...] = jnp.zeros_like(terms)
        for rb in range(blocks):
            rows = pl.ds(rb * width, width)

            @pl.when(row_on[rb])
            def _(rows=rows):
                terms[...] += dot3(split(extra[rows, :]), split(out[rows, :]), ((0,), (0,)))

        @pl.when(table[2 * count + blocks] > 0)
        def _():
            terms[...] += terms[...].T


def product(table, inverse_anc, arrays, slots, width, acc=None, extra=None):
    rows = inverse_anc.shape[0]
    blocks = rows // width
    count = len(slots)
    any_spec = pl.BlockSpec(memory_space=pl.ANY)
    vmem = pl.BlockSpec(memory_space=pltpu.VMEM)
    operands = [pltpu.with_memory_space_constraint(inverse_anc, pltpu.HBM), *arrays]
    specs = [pl.BlockSpec(memory_space=pltpu.HBM)] + [any_spec] * len(arrays)
    for more in (acc, extra):
        if more is not None:
            operands.append(more)
            specs.append(any_spec)
    shapes = [pltpu.HBM((rows, width), jnp.float32)]
    if extra is not None:
        shapes.append(jax.ShapeDtypeStruct((width, width), jnp.float32))
    return pl.pallas_call(
        functools.partial(product_kernel, slots, blocks, width, acc is not None, extra is not None),
        out_shape=shapes,
        grid_spec=pltpu.PrefetchScalarGridSpec(
            num_scalar_prefetch=1,
            grid=(1,),
            in_specs=specs,
            out_specs=[vmem] * len(shapes),
            scratch_shapes=[
                pltpu.VMEM((count, blocks, width, width), jnp.float32),
                pltpu.VMEM((count, width, width), jnp.float32),
                pltpu.VMEM((rows, width), jnp.float32),
                pltpu.SemaphoreType.DMA((count, blocks)),
                pltpu.SemaphoreType.DMA((count,)),
                pltpu.SemaphoreType.DMA((2,)),
            ],
        ),
        compiler_params=pltpu.CompilerParams(vmem_limit_bytes=20 * 1024 * 1024),
        cost_estimate=pl.CostEstimate(
            flops=6 * rows * width * width * count // 4,
            bytes_accessed=4 * rows * width * count // 2,
            transcendentals=0,
        ),
    )(table, *operands)


CORE, X, Z, FAR = 1, 2, 4, 8
FIRST = ((0, 0), (0, 1), (X, 0), (Z, 1), (1, 0), (1, 1), (X | 1, 0), (Z | 1, 1))
SECOND = tuple((m | c, h) for c in (0, 1) for m, h in ((Z, 0), (Z | X, 0), (X, 1), (Z | X, 1)))
WHOLE = tuple((m | c, h) for c in (0, 1) for m in (0, X, Z, Z | X) for h in (0, 1))
SLOTS1 = ((0, 0), (0, 1), (1, 0), (2, 0), (3, 0), (3, 1), (4, 0), (5, 0))
SLOTS2 = ((0, 0), (0, 1), (1, 0), (1, 1), (2, 0), (2, 1), (3, 0), (3, 1))
SLOTSW = tuple((i, h) for i in range(8) for h in (0, 1))
SLOTS12 = SLOTS1 + tuple((6 + i, h) for i, h in SLOTS2)


def local_two(n_row, inverse_anc, lower_panel, structure, diag_inverse):
    n_col = 2
    rows = inverse_anc.shape[0]
    width = diag_inverse.shape[1]
    half = rows // 2
    row, col = lax.axis_index("row"), lax.axis_index("col")
    near = (row // FAR) == col
    every = [(r, c) for r in range(n_row) for c in range(n_col)]

    def is_near(r, c):
        return r // FAR == c

    def move(value, mask, across, who=None):
        pairs = [
            (r * n_col + c, (r ^ mask) * n_col + (c ^ across))
            for r, c in every
            if who is None or is_near(r, c) == who
        ]
        return lax.ppermute(value, BOTH, pairs)

    def table(listed, order, who):
        block = ((row % FAR) ^ jnp.array([m for m, _ in order], jnp.int32)) * 2
        block = block + jnp.array([h for _, h in order], jnp.int32)
        ids = jnp.concatenate([block + col * 2 * FAR, row * 2 + jnp.arange(2, dtype=jnp.int32)])
        on = jnp.any(ids[:, None] == listed[0][None, :], axis=1)
        count = len(order)
        on = on & ((jnp.arange(count + 2) >= count) | (near == who))
        far = jnp.logical_not(near) & jnp.bool_(order == SECOND)
        return jnp.concatenate([block, on.astype(jnp.int32), far.astype(jnp.int32)[None]])

    def step_one(q, who):
        return move(q[:half], X, 0, who), move(q[half:], Z, 0, who)

    def step_two(q, one, who):
        first, second = jnp.concatenate([q[:half], one[0]]), jnp.concatenate([q[half:], one[1]])
        return move(first, Z, 0, who), move(second, X, 0, who)

    def with_sibling(arrays, who):
        return list(arrays) + [move(v, CORE, 0, who) for v in arrays]

    in_hbm = lambda v: pltpu.with_memory_space_constraint(v, pltpu.HBM)
    n_z = move(lower_panel, Z, 0, True)
    n_x = move(lower_panel, X, 0, True)
    got_far = move(lower_panel, FAR, 1, False)
    lower_other = move(lower_panel, 0, 1)
    q_far = move(lower_panel, FAR, 0, True)
    other_structure = move(structure, 0, 1)
    m_x = move(lower_other, X, 0, True)
    m_z = move(lower_other, Z, 0, True)
    n_zx = move(n_z, X, 0, True)
    m_xz = move(m_x, Z, 0, True)
    n_all = with_sibling([lower_panel, n_x, n_z, n_zx], None)
    n_all[0] = in_hbm(lower_panel)
    m_all = with_sibling([lower_other, m_x, m_z], None)
    m_xzs = move(m_xz, CORE, 0, None)
    m_all = m_all[:3] + [m_xz] + m_all[3:] + [m_xzs]
    o_one = step_one(got_far, False)
    o_two = step_two(got_far, o_one, False)
    o_first = with_sibling([got_far, *o_one], None)
    o_second = with_sibling(o_two, None)
    f_one = step_one(q_far, False)
    f_two = step_two(q_far, f_one, False)
    f_first = with_sibling([q_far, *f_one], None)
    f_second = with_sibling(f_two, None)

    own, own_terms = product(
        table(structure, WHOLE, True), inverse_anc, n_all, SLOTSW, width, extra=n_all[0]
    )
    (part,) = product(table(other_structure, WHOLE, True), inverse_anc, m_all, SLOTSW, width)
    (part,) = product(
        table(other_structure, FIRST, False), inverse_anc, o_first, SLOTS1, width,
        acc=in_hbm(part),
    )
    part, other_terms = product(
        table(other_structure, SECOND, False), inverse_anc, o_second, SLOTS2, width,
        acc=in_hbm(part), extra=lower_other,
    )
    recv = move(part, 0, 1)
    (own,) = product(
        table(structure, FIRST + SECOND, False), inverse_anc, f_first + f_second, SLOTS12, width,
        acc=in_hbm(own),
    )
    keep = keep_rows(structure, row * rows, rows, width)
    panel = jnp.where(keep, -(own + recv), jnp.float32(0.0))

    def parts(value, mask):
        size = value.shape[0] // 2
        bit = (row & mask) > 0
        low, high = value[:size], value[size:]
        return jnp.where(bit, high, low), jnp.where(bit, low, high)

    def double(value, mask):
        bit = (row & mask) > 0
        got = move(value, mask, 0)
        return jnp.concatenate([jnp.where(bit, got, value), jnp.where(bit, value, got)])

    u_keep, u_send = parts(own_terms, CORE)
    v_keep, v_send = parts(other_terms, CORE)
    size = u_keep.shape[0]
    got = move(jnp.concatenate([u_send, v_send]), CORE, 0)
    u_keep, u_send = parts(u_keep + got[:size], X)
    v_keep, v_send = parts(v_keep + got[size:], X)
    total = u_keep + move(u_send, X, 0) + move(v_keep, 0, 1) + move(v_send, X, 1)
    total = total + move(total, Z, 0) + move(total, FAR, 0) + move(total, FAR | Z, 0)
    total = double(double(total, X), CORE)
    return panel, diag_inverse + total


def solution(mesh):
    n_row, n_col = mesh.shape["row"], mesh.shape["col"]

    def local(inverse_anc, lower_panel, structure, diag_inverse):
        rows, columns = inverse_anc.shape
        width = diag_inverse.shape[1]
        planned = (
            n_col == 2 and n_row == 2 * FAR and rows == 2 * width
            and structure.shape[0] == 1 and columns == FAR * rows
        )
        if planned:
            return local_two(n_row, inverse_anc, lower_panel, structure, diag_inverse)
        return local_any(inverse_anc, lower_panel, structure, diag_inverse)

    return jax.shard_map(
        local,
        mesh=mesh,
        in_specs=(P("row", "col"), P("row", "col"), P("col", None), P("col", None)),
        out_specs=(P("row", "col"), P("col", None)),
        check_vma=False,
    )
```

```python
import functools

import jax
import jax.numpy as jnp
from jax import lax
from jax.experimental import pallas as pl
from jax.experimental.pallas import tpu as pltpu
from jax.sharding import PartitionSpec as P


BOTH = ("row", "col")


def keep_rows(structure, first_row, row_count, sn_width):
    block_ids = (first_row + jnp.arange(row_count, dtype=jnp.int32)) // sn_width
    listed = jnp.any(structure[None, :, :] == block_ids[:, None, None], axis=2)
    return jnp.repeat(listed, sn_width, axis=1)


def local_any(inverse_anc, lower_panel, structure, diag_inverse):
    local_rows = inverse_anc.shape[0]
    sn_width = diag_inverse.shape[1]
    local_count = structure.shape[0]
    keep = keep_rows(structure, lax.axis_index("row") * local_rows, local_rows, sn_width)
    masked = jnp.where(keep, lower_panel, jnp.float32(0.0))
    rows = lax.all_gather(masked, "row", axis=0, tiled=True)
    rows = lax.all_to_all(rows, "col", split_axis=0, concat_axis=1, tiled=True)
    part = jnp.dot(inverse_anc, rows, precision=lax.Precision.HIGHEST)
    product = lax.psum_scatter(part, "col", scatter_dimension=1, tiled=True)
    panel = jnp.where(keep, -product, jnp.float32(0.0))
    terms = jnp.einsum(
        "ika,ikb->kab",
        masked.reshape(local_rows, local_count, sn_width),
        panel.reshape(local_rows, local_count, sn_width),
        precision=lax.Precision.HIGHEST,
    )
    total = lax.psum(terms.reshape(local_count * sn_width, sn_width), "row")
    return panel, diag_inverse - total


def split(value):
    high = value.astype(jnp.bfloat16)
    low = (value - high.astype(jnp.float32)).astype(jnp.bfloat16)
    return high, low


def dot3(a, b, dims):
    dot = lambda u, v: lax.dot_general(u, v, (dims, ((), ())), preferred_element_type=jnp.float32)
    return dot(a[0], b[0]) + (dot(a[0], b[1]) + dot(a[1], b[0]))


def product_kernel(slots, blocks, width, has_acc, final, table, *refs):
    count = len(slots)
    narrays = 1 + max(s[0] for s in slots)
    refs = list(refs)
    a_hbm = refs.pop(0)
    arrays = [refs.pop(0) for _ in range(narrays)]
    acc_in = refs.pop(0) if has_acc else None
    extra_in = refs.pop(0) if final else None
    out = refs.pop(0)
    terms = refs.pop(0) if final else None
    a_buf, p_buf, extra, a_sem, p_sem, one_sem = refs
    row_on = [table[2 * count + rb] > 0 for rb in range(blocks)]
    all_on = functools.reduce(jnp.logical_and, row_on)
    dot = functools.partial(jnp.dot, preferred_element_type=jnp.float32)

    def a_copy(p, rb):
        return pltpu.make_async_copy(
            a_hbm.at[pl.ds(rb * width, width), pl.ds(pl.multiple_of(table[p] * width, width), width)],
            a_buf.at[p, rb],
            a_sem.at[p, rb],
        )

    def p_copy(p):
        array, at = slots[p]
        return pltpu.make_async_copy(arrays[array].at[pl.ds(at * width, width), :], p_buf.at[p], p_sem.at[p])

    if has_acc:
        acc_copy = pltpu.make_async_copy(acc_in, out, one_sem.at[0])
        acc_copy.start()
    for p in range(count):
        @pl.when(table[count + p] > 0)
        def _(p=p):
            p_copy(p).start()
            for rb in range(blocks):
                @pl.when(row_on[rb])
                def _(rb=rb):
                    a_copy(p, rb).start()

    if final:
        extra_copy = pltpu.make_async_copy(extra_in, extra, one_sem.at[1])
        extra_copy.start()
    if has_acc:
        acc_copy.wait()
    else:
        out[...] = jnp.zeros_like(out)

    def step(p, carry):
        @pl.when(table[count + p] > 0)
        def _():
            pltpu.make_async_copy(p_buf.at[p], p_buf.at[p], p_sem.at[p]).wait()
            high, low = split(p_buf[p])

            def add(first, size):
                for rb in range(first, first + size):
                    a_copy(p, rb).wait()
                a_high, a_low = split(a_buf[p, first : first + size].reshape(size * width, width))
                both = dot(jnp.concatenate([a_high, a_low]), high)
                total = both[: size * width] + (both[size * width :] + dot(a_high, low))
                out[pl.ds(first * width, size * width), :] += total

            @pl.when(all_on)
            def _():
                add(0, blocks)

            for rb in range(blocks):
                @pl.when(jnp.logical_not(all_on) & row_on[rb])
                def _(rb=rb):
                    add(rb, 1)

        return carry

    lax.fori_loop(0, count, step, 0)
    if final:
        extra_copy.wait()
        terms[...] = jnp.zeros_like(terms)
        for rb in range(blocks):
            rows = pl.ds(rb * width, width)

            @pl.when(row_on[rb])
            def _(rows=rows):
                terms[...] += dot3(split(extra[rows, :]), split(out[rows, :]), ((0,), (0,)))

        @pl.when(table[2 * count + blocks] > 0)
        def _():
            terms[...] += terms[...].T


def product(table, inverse_anc, arrays, slots, width, acc=None, extra=None):
    rows = inverse_anc.shape[0]
    blocks = rows // width
    count = len(slots)
    any_spec = pl.BlockSpec(memory_space=pl.ANY)
    vmem = pl.BlockSpec(memory_space=pltpu.VMEM)
    operands = [pltpu.with_memory_space_constraint(inverse_anc, pltpu.HBM), *arrays]
    specs = [pl.BlockSpec(memory_space=pltpu.HBM)] + [any_spec] * len(arrays)
    for more in (acc, extra):
        if more is not None:
            operands.append(more)
            specs.append(any_spec)
    shapes = [pltpu.HBM((rows, width), jnp.float32)]
    if extra is not None:
        shapes.append(jax.ShapeDtypeStruct((width, width), jnp.float32))
    return pl.pallas_call(
        functools.partial(product_kernel, slots, blocks, width, acc is not None, extra is not None),
        out_shape=shapes,
        grid_spec=pltpu.PrefetchScalarGridSpec(
            num_scalar_prefetch=1,
            grid=(1,),
            in_specs=specs,
            out_specs=[vmem] * len(shapes),
            scratch_shapes=[
                pltpu.VMEM((count, blocks, width, width), jnp.float32),
                pltpu.VMEM((count, width, width), jnp.float32),
                pltpu.VMEM((rows, width), jnp.float32),
                pltpu.SemaphoreType.DMA((count, blocks)),
                pltpu.SemaphoreType.DMA((count,)),
                pltpu.SemaphoreType.DMA((2,)),
            ],
        ),
        compiler_params=pltpu.CompilerParams(vmem_limit_bytes=20 * 1024 * 1024),
        cost_estimate=pl.CostEstimate(
            flops=6 * rows * width * width * count // 4,
            bytes_accessed=4 * rows * width * count // 2,
            transcendentals=0,
        ),
    )(table, *operands)


CORE, X, Z, FAR = 1, 2, 4, 8
FIRST = ((0, 0), (0, 1), (X, 0), (Z, 1), (1, 0), (1, 1), (X | 1, 0), (Z | 1, 1))
SECOND = tuple((m | c, h) for c in (0, 1) for m, h in ((Z, 0), (Z | X, 0), (X, 1), (Z | X, 1)))
SLOTS1 = ((0, 0), (0, 1), (1, 0), (2, 0), (3, 0), (3, 1), (4, 0), (5, 0))
SLOTS2 = ((0, 0), (0, 1), (1, 0), (1, 1), (2, 0), (2, 1), (3, 0), (3, 1))
SLOTS12 = SLOTS1 + tuple((6 + i, h) for i, h in SLOTS2)


def local_two(n_row, inverse_anc, lower_panel, structure, diag_inverse):
    n_col = 2
    rows = inverse_anc.shape[0]
    width = diag_inverse.shape[1]
    half = rows // 2
    row, col = lax.axis_index("row"), lax.axis_index("col")
    near = (row // FAR) == col
    every = [(r, c) for r in range(n_row) for c in range(n_col)]

    def is_near(r, c):
        return r // FAR == c

    def move(value, mask, across, who=None):
        pairs = [
            (r * n_col + c, (r ^ mask) * n_col + (c ^ across))
            for r, c in every
            if who is None or is_near(r, c) == who
        ]
        return lax.ppermute(value, BOTH, pairs)

    def table(listed, order, who):
        block = ((row % FAR) ^ jnp.array([m for m, _ in order], jnp.int32)) * 2
        block = block + jnp.array([h for _, h in order], jnp.int32)
        ids = jnp.concatenate([block + col * 2 * FAR, row * 2 + jnp.arange(2, dtype=jnp.int32)])
        on = jnp.any(ids[:, None] == listed[0][None, :], axis=1)
        count = len(order)
        if who is not None:
            on = on & ((jnp.arange(count + 2) >= count) | (near == who))
        far = jnp.logical_not(near) if who is None else jnp.zeros((), jnp.bool_)
        return jnp.concatenate([block, on.astype(jnp.int32), far.astype(jnp.int32)[None]])

    def step_one(q, who):
        return move(q[:half], X, 0, who), move(q[half:], Z, 0, who)

    def step_two(q, one, who):
        first, second = jnp.concatenate([q[:half], one[0]]), jnp.concatenate([q[half:], one[1]])
        return move(first, Z, 0, who), move(second, X, 0, who)

    def with_sibling(arrays, who):
        return list(arrays) + [move(v, CORE, 0, who) for v in arrays]

    other_structure = move(structure, 0, 1)
    got_far = move(lower_panel, FAR, 1, False)
    lower_other = move(lower_panel, 0, 1)
    n_one = step_one(lower_panel, True)
    q_far = move(lower_panel, FAR, 0, True)
    n_two = step_two(lower_panel, n_one, True)
    in_hbm = lambda v: pltpu.with_memory_space_constraint(v, pltpu.HBM)
    n_first = with_sibling([lower_panel, *n_one], None)
    n_first[0] = in_hbm(lower_panel)
    n_second = with_sibling(n_two, None)
    q_other = jnp.where(near, lower_other, got_far)
    o_one = step_one(q_other, None)
    o_two = step_two(q_other, o_one, None)
    o_first = with_sibling([q_other, *o_one], None)
    o_second = with_sibling(o_two, None)
    f_one = step_one(q_far, False)
    f_two = step_two(q_far, f_one, False)
    f_first = with_sibling([q_far, *f_one], None)
    f_second = with_sibling(f_two, None)

    own, own_terms = product(
        table(structure, FIRST + SECOND, True), inverse_anc, n_first + n_second, SLOTS12, width,
        extra=n_first[0],
    )
    (part,) = product(table(other_structure, FIRST, None), inverse_anc, o_first, SLOTS1, width)
    part, other_terms = product(
        table(other_structure, SECOND, None), inverse_anc, o_second, SLOTS2, width,
        acc=in_hbm(part), extra=lower_other,
    )
    recv = move(part, 0, 1)
    (own,) = product(
        table(structure, FIRST + SECOND, False), inverse_anc, f_first + f_second, SLOTS12, width,
        acc=in_hbm(own),
    )
    keep = keep_rows(structure, row * rows, rows, width)
    panel = jnp.where(keep, -(own + recv), jnp.float32(0.0))

    def parts(value, mask):
        size = value.shape[0] // 2
        bit = (row & mask) > 0
        low, high = value[:size], value[size:]
        return jnp.where(bit, high, low), jnp.where(bit, low, high)

    def double(value, mask):
        bit = (row & mask) > 0
        got = move(value, mask, 0)
        return jnp.concatenate([jnp.where(bit, got, value), jnp.where(bit, value, got)])

    u_keep, u_send = parts(own_terms, CORE)
    v_keep, v_send = parts(other_terms, CORE)
    size = u_keep.shape[0]
    got = move(jnp.concatenate([u_send, v_send]), CORE, 0)
    u_keep, u_send = parts(u_keep + got[:size], X)
    v_keep, v_send = parts(v_keep + got[size:], X)
    total = u_keep + move(u_send, X, 0) + move(v_keep, 0, 1) + move(v_send, X, 1)
    total = total + move(total, Z, 0) + move(total, FAR, 0) + move(total, FAR | Z, 0)
    total = double(double(total, X), CORE)
    return panel, diag_inverse + total


def solution(mesh):
    n_row, n_col = mesh.shape["row"], mesh.shape["col"]

    def local(inverse_anc, lower_panel, structure, diag_inverse):
        rows, columns = inverse_anc.shape
        width = diag_inverse.shape[1]
        planned = (
            n_col == 2 and n_row == 2 * FAR and rows == 2 * width
            and structure.shape[0] == 1 and columns == FAR * rows
        )
        if planned:
            return local_two(n_row, inverse_anc, lower_panel, structure, diag_inverse)
        return local_any(inverse_anc, lower_panel, structure, diag_inverse)

    return jax.shard_map(
        local,
        mesh=mesh,
        in_specs=(P("row", "col"), P("row", "col"), P("col", None), P("col", None)),
        out_specs=(P("row", "col"), P("col", None)),
        check_vma=False,
    )
```

```python
import functools

import jax
import jax.numpy as jnp
from jax import lax
from jax.experimental import pallas as pl
from jax.experimental.pallas import tpu as pltpu
from jax.sharding import PartitionSpec as P


BOTH = ("row", "col")


def keep_rows(structure, first_row, row_count, sn_width):
    block_ids = (first_row + jnp.arange(row_count, dtype=jnp.int32)) // sn_width
    listed = jnp.any(structure[None, :, :] == block_ids[:, None, None], axis=2)
    return jnp.repeat(listed, sn_width, axis=1)


def local_any(inverse_anc, lower_panel, structure, diag_inverse):
    local_rows = inverse_anc.shape[0]
    sn_width = diag_inverse.shape[1]
    local_count = structure.shape[0]
    keep = keep_rows(structure, lax.axis_index("row") * local_rows, local_rows, sn_width)
    masked = jnp.where(keep, lower_panel, jnp.float32(0.0))
    rows = lax.all_gather(masked, "row", axis=0, tiled=True)
    rows = lax.all_to_all(rows, "col", split_axis=0, concat_axis=1, tiled=True)
    part = jnp.dot(inverse_anc, rows, precision=lax.Precision.HIGHEST)
    product = lax.psum_scatter(part, "col", scatter_dimension=1, tiled=True)
    panel = jnp.where(keep, -product, jnp.float32(0.0))
    terms = jnp.einsum(
        "ika,ikb->kab",
        masked.reshape(local_rows, local_count, sn_width),
        panel.reshape(local_rows, local_count, sn_width),
        precision=lax.Precision.HIGHEST,
    )
    total = lax.psum(terms.reshape(local_count * sn_width, sn_width), "row")
    return panel, diag_inverse - total


def split(value):
    high = value.astype(jnp.bfloat16)
    low = (value - high.astype(jnp.float32)).astype(jnp.bfloat16)
    return high, low


def dot3(a, b, dims):
    dot = lambda u, v: lax.dot_general(u, v, (dims, ((), ())), preferred_element_type=jnp.float32)
    return dot(a[0], b[0]) + (dot(a[0], b[1]) + dot(a[1], b[0]))


def product_kernel(slots, blocks, width, has_acc, final, table, *refs):
    count = len(slots)
    narrays = 1 + max(s[0] for s in slots)
    refs = list(refs)
    a_hbm = refs.pop(0)
    arrays = [refs.pop(0) for _ in range(narrays)]
    acc_in = refs.pop(0) if has_acc else None
    extra_in = refs.pop(0) if final else None
    out = refs.pop(0)
    terms = refs.pop(0) if final else None
    a_buf, p_buf, extra, a_sem, p_sem, one_sem = refs
    row_on = [table[2 * count + rb] > 0 for rb in range(blocks)]
    all_on = functools.reduce(jnp.logical_and, row_on)
    dot = functools.partial(jnp.dot, preferred_element_type=jnp.float32)

    held = a_buf.shape[0]

    def a_copy(p, rb):
        return pltpu.make_async_copy(
            a_hbm.at[pl.ds(rb * width, width), pl.ds(pl.multiple_of(table[p] * width, width), width)],
            a_buf.at[lax.rem(p, held), rb],
            a_sem.at[lax.rem(p, held), rb],
        )

    def start(p):
        array, at = slots[p]

        @pl.when(table[count + p] > 0)
        def _():
            pltpu.make_async_copy(
                arrays[array].at[pl.ds(at * width, width), :], p_buf.at[p % held], p_sem.at[p % held]
            ).start()
            for rb in range(blocks):
                @pl.when(row_on[rb])
                def _(rb=rb):
                    a_copy(p, rb).start()

    if has_acc:
        acc_copy = pltpu.make_async_copy(acc_in, out, one_sem.at[0])
        acc_copy.start()
    for p in range(held):
        start(p)
    if final:
        extra_copy = pltpu.make_async_copy(extra_in, extra, one_sem.at[1])
        extra_copy.start()
    if has_acc:
        acc_copy.wait()
    else:
        out[...] = jnp.zeros_like(out)

    def step(p, carry):
        @pl.when(table[count + p] > 0)
        def _():
            slot = lax.rem(p, held)
            pltpu.make_async_copy(p_buf.at[slot], p_buf.at[slot], p_sem.at[slot]).wait()
            high, low = split(p_buf[slot])

            def add(first, size):
                for rb in range(first, first + size):
                    a_copy(p, rb).wait()
                a_high, a_low = split(a_buf[slot, first : first + size].reshape(size * width, width))
                both = dot(jnp.concatenate([a_high, a_low]), high)
                total = both[: size * width] + (both[size * width :] + dot(a_high, low))
                out[pl.ds(first * width, size * width), :] += total

            @pl.when(all_on)
            def _():
                add(0, blocks)

            for rb in range(blocks):
                @pl.when(jnp.logical_not(all_on) & row_on[rb])
                def _(rb=rb):
                    add(rb, 1)

        for later in range(held, count):
            @pl.when(p == later - held)
            def _(later=later):
                start(later)

        return carry

    lax.fori_loop(0, count, step, 0)
    if final:
        extra_copy.wait()
        terms[...] = jnp.zeros_like(terms)
        for rb in range(blocks):
            rows = pl.ds(rb * width, width)

            @pl.when(row_on[rb])
            def _(rows=rows):
                terms[...] += dot3(split(extra[rows, :]), split(out[rows, :]), ((0,), (0,)))

        @pl.when(table[2 * count + blocks] > 0)
        def _():
            terms[...] += terms[...].T


def product(table, inverse_anc, arrays, slots, width, acc=None, extra=None):
    rows = inverse_anc.shape[0]
    blocks = rows // width
    count = len(slots)
    held = min(count, 8)
    any_spec = pl.BlockSpec(memory_space=pl.ANY)
    vmem = pl.BlockSpec(memory_space=pltpu.VMEM)
    operands = [pltpu.with_memory_space_constraint(inverse_anc, pltpu.HBM), *arrays]
    specs = [pl.BlockSpec(memory_space=pltpu.HBM)] + [any_spec] * len(arrays)
    for more in (acc, extra):
        if more is not None:
            operands.append(more)
            specs.append(any_spec)
    shapes = [pltpu.HBM((rows, width), jnp.float32)]
    if extra is not None:
        shapes.append(jax.ShapeDtypeStruct((width, width), jnp.float32))
    return pl.pallas_call(
        functools.partial(product_kernel, slots, blocks, width, acc is not None, extra is not None),
        out_shape=shapes,
        grid_spec=pltpu.PrefetchScalarGridSpec(
            num_scalar_prefetch=1,
            grid=(1,),
            in_specs=specs,
            out_specs=[vmem] * len(shapes),
            scratch_shapes=[
                pltpu.VMEM((held, blocks, width, width), jnp.float32),
                pltpu.VMEM((held, width, width), jnp.float32),
                pltpu.VMEM((rows, width), jnp.float32),
                pltpu.SemaphoreType.DMA((held, blocks)),
                pltpu.SemaphoreType.DMA((held,)),
                pltpu.SemaphoreType.DMA((2,)),
            ],
        ),
        compiler_params=pltpu.CompilerParams(vmem_limit_bytes=12 * 1024 * 1024),
        cost_estimate=pl.CostEstimate(
            flops=6 * rows * width * width * count // 4,
            bytes_accessed=4 * rows * width * count // 2,
            transcendentals=0,
        ),
    )(table, *operands)


CORE, X, Z, FAR = 1, 2, 4, 8
FIRST = ((0, 0), (0, 1), (X, 0), (Z, 1), (1, 0), (1, 1), (X | 1, 0), (Z | 1, 1))
SECOND = tuple((m | c, h) for c in (0, 1) for m, h in ((Z, 0), (Z | X, 0), (X, 1), (Z | X, 1)))
SLOTS1 = ((0, 0), (0, 1), (1, 0), (2, 0), (3, 0), (3, 1), (4, 0), (5, 0))
SLOTS2 = ((0, 0), (0, 1), (1, 0), (1, 1), (2, 0), (2, 1), (3, 0), (3, 1))
SLOTS12 = SLOTS1 + tuple((6 + i, h) for i, h in SLOTS2)


def local_two(n_row, inverse_anc, lower_panel, structure, diag_inverse):
    n_col = 2
    rows = inverse_anc.shape[0]
    width = diag_inverse.shape[1]
    half = rows // 2
    row, col = lax.axis_index("row"), lax.axis_index("col")
    near = (row // FAR) == col
    every = [(r, c) for r in range(n_row) for c in range(n_col)]

    def is_near(r, c):
        return r // FAR == c

    def move(value, mask, across, who=None):
        pairs = [
            (r * n_col + c, (r ^ mask) * n_col + (c ^ across))
            for r, c in every
            if who is None or is_near(r, c) == who
        ]
        return lax.ppermute(value, BOTH, pairs)

    def table(listed, order, who):
        block = ((row % FAR) ^ jnp.array([m for m, _ in order], jnp.int32)) * 2
        block = block + jnp.array([h for _, h in order], jnp.int32)
        ids = jnp.concatenate([block + col * 2 * FAR, row * 2 + jnp.arange(2, dtype=jnp.int32)])
        on = jnp.any(ids[:, None] == listed[0][None, :], axis=1)
        if who is not None:
            on = on & (near == who)
        far = jnp.logical_not(near) if who is None else jnp.zeros((), jnp.bool_)
        return jnp.concatenate([block, on.astype(jnp.int32), far.astype(jnp.int32)[None]])

    def step_one(q, who):
        return move(q[:half], X, 0, who), move(q[half:], Z, 0, who)

    def step_two(q, one, who):
        first, second = jnp.concatenate([q[:half], one[0]]), jnp.concatenate([q[half:], one[1]])
        return move(first, Z, 0, who), move(second, X, 0, who)

    def with_sibling(arrays, who):
        return list(arrays) + [move(v, CORE, 0, who) for v in arrays]

    other_structure = move(structure, 0, 1)
    got_far = move(lower_panel, FAR, 1, False)
    lower_other = move(lower_panel, 0, 1)
    n_one = step_one(lower_panel, True)
    q_far = move(lower_panel, FAR, 0, True)
    n_two = step_two(lower_panel, n_one, True)
    in_hbm = lambda v: pltpu.with_memory_space_constraint(v, pltpu.HBM)
    n_first = with_sibling([lower_panel, *n_one], None)
    n_first[0] = in_hbm(lower_panel)
    n_second = with_sibling(n_two, None)
    q_other = jnp.where(near, lower_other, got_far)
    o_one = step_one(q_other, None)
    o_two = step_two(q_other, o_one, None)
    o_first = with_sibling([q_other, *o_one], None)
    o_second = with_sibling(o_two, None)
    f_one = step_one(q_far, False)
    f_two = step_two(q_far, f_one, False)
    f_first = with_sibling([q_far, *f_one], None)
    f_second = with_sibling(f_two, None)

    own, own_terms = product(
        table(structure, FIRST + SECOND, True), inverse_anc, n_first + n_second, SLOTS12, width,
        extra=n_first[0],
    )
    (part,) = product(table(other_structure, FIRST, None), inverse_anc, o_first, SLOTS1, width)
    part, other_terms = product(
        table(other_structure, SECOND, None), inverse_anc, o_second, SLOTS2, width,
        acc=in_hbm(part), extra=lower_other,
    )
    recv = move(part, 0, 1)
    (own,) = product(
        table(structure, FIRST + SECOND, False), inverse_anc, f_first + f_second, SLOTS12, width,
        acc=in_hbm(own),
    )
    keep = keep_rows(structure, row * rows, rows, width)
    panel = jnp.where(keep, -(own + recv), jnp.float32(0.0))

    def parts(value, mask):
        size = value.shape[0] // 2
        bit = (row & mask) > 0
        low, high = value[:size], value[size:]
        return jnp.where(bit, high, low), jnp.where(bit, low, high)

    def double(value, mask):
        bit = (row & mask) > 0
        got = move(value, mask, 0)
        return jnp.concatenate([jnp.where(bit, got, value), jnp.where(bit, value, got)])

    u_keep, u_send = parts(own_terms, CORE)
    v_keep, v_send = parts(other_terms, CORE)
    size = u_keep.shape[0]
    got = move(jnp.concatenate([u_send, v_send]), CORE, 0)
    u_keep, u_send = parts(u_keep + got[:size], X)
    v_keep, v_send = parts(v_keep + got[size:], X)
    total = u_keep + move(u_send, X, 0) + move(v_keep, 0, 1) + move(v_send, X, 1)
    total = total + move(total, Z, 0) + move(total, FAR, 0) + move(total, FAR | Z, 0)
    total = double(double(total, X), CORE)
    return panel, diag_inverse + total


def solution(mesh):
    n_row, n_col = mesh.shape["row"], mesh.shape["col"]

    def local(inverse_anc, lower_panel, structure, diag_inverse):
        rows, columns = inverse_anc.shape
        width = diag_inverse.shape[1]
        planned = (
            n_col == 2 and n_row == 2 * FAR and rows == 2 * width
            and structure.shape[0] == 1 and columns == FAR * rows
        )
        if planned:
            return local_two(n_row, inverse_anc, lower_panel, structure, diag_inverse)
        return local_any(inverse_anc, lower_panel, structure, diag_inverse)

    return jax.shard_map(
        local,
        mesh=mesh,
        in_specs=(P("row", "col"), P("row", "col"), P("col", None), P("col", None)),
        out_specs=(P("row", "col"), P("col", None)),
        check_vma=False,
    )
```

```python
import functools

import jax
import jax.numpy as jnp
from jax import lax
from jax.experimental import pallas as pl
from jax.experimental.pallas import tpu as pltpu
from jax.sharding import PartitionSpec as P


BOTH = ("row", "col")


def keep_rows(structure, first_row, row_count, sn_width):
    block_ids = (first_row + jnp.arange(row_count, dtype=jnp.int32)) // sn_width
    listed = jnp.any(structure[None, :, :] == block_ids[:, None, None], axis=2)
    return jnp.repeat(listed, sn_width, axis=1)


def local_any(inverse_anc, lower_panel, structure, diag_inverse):
    local_rows = inverse_anc.shape[0]
    sn_width = diag_inverse.shape[1]
    local_count = structure.shape[0]
    keep = keep_rows(structure, lax.axis_index("row") * local_rows, local_rows, sn_width)
    masked = jnp.where(keep, lower_panel, jnp.float32(0.0))
    rows = lax.all_gather(masked, "row", axis=0, tiled=True)
    rows = lax.all_to_all(rows, "col", split_axis=0, concat_axis=1, tiled=True)
    part = jnp.dot(inverse_anc, rows, precision=lax.Precision.HIGHEST)
    product = lax.psum_scatter(part, "col", scatter_dimension=1, tiled=True)
    panel = jnp.where(keep, -product, jnp.float32(0.0))
    terms = jnp.einsum(
        "ika,ikb->kab",
        masked.reshape(local_rows, local_count, sn_width),
        panel.reshape(local_rows, local_count, sn_width),
        precision=lax.Precision.HIGHEST,
    )
    total = lax.psum(terms.reshape(local_count * sn_width, sn_width), "row")
    return panel, diag_inverse - total


def split(value):
    high = value.astype(jnp.bfloat16)
    low = (value - high.astype(jnp.float32)).astype(jnp.bfloat16)
    return high, low


def dot3(a, b, dims):
    dot = lambda u, v: lax.dot_general(u, v, (dims, ((), ())), preferred_element_type=jnp.float32)
    return dot(a[0], b[0]) + (dot(a[0], b[1]) + dot(a[1], b[0]))


def product_kernel(slots, blocks, width, has_acc, final, table, *refs):
    count = len(slots)
    narrays = 1 + max(s[0] for s in slots)
    refs = list(refs)
    a_hbm = refs.pop(0)
    arrays = [refs.pop(0) for _ in range(narrays)]
    acc_in = refs.pop(0) if has_acc else None
    extra_in = refs.pop(0) if final else None
    out = refs.pop(0)
    terms = refs.pop(0) if final else None
    a_buf, p_buf, extra, a_sem, p_sem, one_sem = refs
    row_on = [table[2 * count + rb] > 0 for rb in range(blocks)]
    all_on = functools.reduce(jnp.logical_and, row_on)
    dot = functools.partial(jnp.dot, preferred_element_type=jnp.float32)

    held = a_buf.shape[0]

    def a_copy(p, rb):
        return pltpu.make_async_copy(
            a_hbm.at[pl.ds(rb * width, width), pl.ds(pl.multiple_of(table[p] * width, width), width)],
            a_buf.at[p % held, rb],
            a_sem.at[p % held, rb],
        )

    def start(p):
        array, at = slots[p]

        @pl.when(table[count + p] > 0)
        def _():
            pltpu.make_async_copy(
                arrays[array].at[pl.ds(at * width, width), :], p_buf.at[p % held], p_sem.at[p % held]
            ).start()
            for rb in range(blocks):
                @pl.when(row_on[rb])
                def _(rb=rb):
                    a_copy(p, rb).start()

    if has_acc:
        acc_copy = pltpu.make_async_copy(acc_in, out, one_sem.at[0])
        acc_copy.start()
    for p in range(held):
        start(p)
    if final:
        extra_copy = pltpu.make_async_copy(extra_in, extra, one_sem.at[1])
        extra_copy.start()
    if has_acc:
        acc_copy.wait()
    else:
        out[...] = jnp.zeros_like(out)

    def step(p, carry):
        @pl.when(table[count + p] > 0)
        def _():
            slot = p % held
            pltpu.make_async_copy(p_buf.at[slot], p_buf.at[slot], p_sem.at[slot]).wait()
            high, low = split(p_buf[slot])

            def add(first, size):
                for rb in range(first, first + size):
                    a_copy(p, rb).wait()
                a_high, a_low = split(a_buf[slot, first : first + size].reshape(size * width, width))
                both = dot(jnp.concatenate([a_high, a_low]), high)
                total = both[: size * width] + (both[size * width :] + dot(a_high, low))
                out[pl.ds(first * width, size * width), :] += total

            @pl.when(all_on)
            def _():
                add(0, blocks)

            for rb in range(blocks):
                @pl.when(jnp.logical_not(all_on) & row_on[rb])
                def _(rb=rb):
                    add(rb, 1)

        for later in range(held, count):
            @pl.when(p == later - held)
            def _(later=later):
                start(later)

        return carry

    if count > 4:
        lax.fori_loop(0, count, step, 0)
    else:
        for p in range(count):
            step(p, 0)
    if final:
        extra_copy.wait()
        terms[...] = jnp.zeros_like(terms)
        for rb in range(blocks):
            rows = pl.ds(rb * width, width)

            @pl.when(row_on[rb])
            def _(rows=rows):
                terms[...] += dot3(split(extra[rows, :]), split(out[rows, :]), ((0,), (0,)))

        @pl.when(table[2 * count + blocks] > 0)
        def _():
            terms[...] += terms[...].T


def product(table, inverse_anc, arrays, slots, width, acc=None, extra=None, kind=jax.ShapeDtypeStruct):
    rows = inverse_anc.shape[0]
    blocks = rows // width
    count = len(slots)
    held = count
    any_spec = pl.BlockSpec(memory_space=pl.ANY)
    vmem = pl.BlockSpec(memory_space=pltpu.VMEM)
    operands = [pltpu.with_memory_space_constraint(inverse_anc, pltpu.HBM), *arrays]
    specs = [pl.BlockSpec(memory_space=pltpu.HBM)] + [any_spec] * len(arrays)
    for more in (acc, extra):
        if more is not None:
            operands.append(more)
            specs.append(any_spec)
    shapes = [kind((rows, width), jnp.float32)]
    if extra is not None:
        shapes.append(jax.ShapeDtypeStruct((width, width), jnp.float32))
    return pl.pallas_call(
        functools.partial(product_kernel, slots, blocks, width, acc is not None, extra is not None),
        out_shape=shapes,
        grid_spec=pltpu.PrefetchScalarGridSpec(
            num_scalar_prefetch=1,
            grid=(1,),
            in_specs=specs,
            out_specs=[vmem] * len(shapes),
            scratch_shapes=[
                pltpu.VMEM((held, blocks, width, width), jnp.float32),
                pltpu.VMEM((held, width, width), jnp.float32),
                pltpu.VMEM((rows, width), jnp.float32),
                pltpu.SemaphoreType.DMA((held, blocks)),
                pltpu.SemaphoreType.DMA((held,)),
                pltpu.SemaphoreType.DMA((2,)),
            ],
        ),
        compiler_params=pltpu.CompilerParams(vmem_limit_bytes=20 * 1024 * 1024),
        cost_estimate=pl.CostEstimate(
            flops=6 * rows * width * width * count // 4,
            bytes_accessed=4 * rows * width * count // 2,
            transcendentals=0,
        ),
    )(table, *operands)


CORE, X, Z, FAR = 1, 2, 4, 8
FIRST = tuple((m | c, h) for c in (0, 1) for m in (0, X, Z) for h in (0, 1))
SECOND = tuple((Z | X | c, h) for c in (0, 1) for h in (0, 1))
SLOTS1 = tuple((i, h) for i in range(6) for h in (0, 1))
SLOTS2 = tuple((i, 0) for i in range(4))
SLOTS12 = SLOTS1 + tuple((6 + i, 0) for i in range(4))


def local_two(n_row, inverse_anc, lower_panel, structure, diag_inverse):
    n_col = 2
    rows = inverse_anc.shape[0]
    width = diag_inverse.shape[1]
    half = rows // 2
    row, col = lax.axis_index("row"), lax.axis_index("col")
    near = (row // FAR) == col
    every = [(r, c) for r in range(n_row) for c in range(n_col)]

    def is_near(r, c):
        return r // FAR == c

    def move(value, mask, across, who=None):
        pairs = [
            (r * n_col + c, (r ^ mask) * n_col + (c ^ across))
            for r, c in every
            if who is None or is_near(r, c) == who
        ]
        return lax.ppermute(value, BOTH, pairs)

    def table(listed, order, who):
        block = ((row % FAR) ^ jnp.array([m for m, _ in order], jnp.int32)) * 2
        block = block + jnp.array([h for _, h in order], jnp.int32)
        ids = jnp.concatenate([block + col * 2 * FAR, row * 2 + jnp.arange(2, dtype=jnp.int32)])
        on = jnp.any(ids[:, None] == listed[0][None, :], axis=1)
        if who is not None:
            on = on & (near == who)
        far = jnp.logical_not(near) if who is None else jnp.zeros((), jnp.bool_)
        return jnp.concatenate([block, on.astype(jnp.int32), far.astype(jnp.int32)[None]])

    def step_one(q, who):
        return move(q, X, 0, who), move(q, Z, 0, who)

    def step_two(one, who):
        z2 = move(one[0][:half], Z, 0, who)
        return z2, move(one[1][half:], X, 0, who)

    def with_sibling(arrays, who):
        return list(arrays) + [move(v, CORE, 0, who) for v in arrays]

    other_structure = move(structure, 0, 1)
    got_far = move(lower_panel, FAR, 1, False)
    lower_other = move(lower_panel, 0, 1)
    n_one = step_one(lower_panel, True)
    q_far = move(lower_panel, FAR, 0, True)
    n_two = step_two(n_one, True)
    in_hbm = lambda v: pltpu.with_memory_space_constraint(v, pltpu.HBM)
    n_first = with_sibling([lower_panel, *n_one], None)
    n_first[0] = in_hbm(lower_panel)
    n_second = with_sibling(n_two, None)
    q_other = jnp.where(near, lower_other, got_far)
    o_one = step_one(q_other, None)
    o_two = step_two(o_one, None)
    o_first = with_sibling([q_other, *o_one], None)
    o_second = with_sibling(o_two, None)
    f_one = step_one(q_far, False)
    f_two = step_two(f_one, False)
    f_first = with_sibling([q_far, *f_one], None)
    f_second = with_sibling(f_two, None)

    own, own_terms = product(
        table(structure, FIRST + SECOND, True), inverse_anc, n_first + n_second, SLOTS12, width,
        extra=n_first[0], kind=pltpu.HBM,
    )
    (part,) = product(table(other_structure, FIRST, None), inverse_anc, o_first, SLOTS1, width)
    part, other_terms = product(
        table(other_structure, SECOND, None), inverse_anc, o_second, SLOTS2, width,
        acc=part, extra=lower_other, kind=pltpu.HBM,
    )
    recv = move(part, 0, 1)
    (own,) = product(
        table(structure, FIRST + SECOND, False), inverse_anc, f_first + f_second, SLOTS12, width,
        acc=in_hbm(own),
    )
    keep = keep_rows(structure, row * rows, rows, width)
    panel = jnp.where(keep, -(own + recv), jnp.float32(0.0))

    def parts(value, mask):
        size = value.shape[0] // 2
        bit = (row & mask) > 0
        low, high = value[:size], value[size:]
        return jnp.where(bit, high, low), jnp.where(bit, low, high)

    def double(value, mask):
        bit = (row & mask) > 0
        got = move(value, mask, 0)
        return jnp.concatenate([jnp.where(bit, got, value), jnp.where(bit, value, got)])

    u_keep, u_send = parts(own_terms, CORE)
    v_keep, v_send = parts(other_terms, CORE)
    size = u_keep.shape[0]
    got = move(jnp.concatenate([u_send, v_send]), CORE, 0)
    u_keep, u_send = parts(u_keep + got[:size], X)
    v_keep, v_send = parts(v_keep + got[size:], X)
    total = u_keep + move(u_send, X, 0) + move(v_keep, 0, 1) + move(v_send, X, 1)
    total = total + move(total, Z, 0) + move(total, FAR, 0) + move(total, FAR | Z, 0)
    total = double(double(total, X), CORE)
    return panel, diag_inverse + total


def solution(mesh):
    n_row, n_col = mesh.shape["row"], mesh.shape["col"]

    def local(inverse_anc, lower_panel, structure, diag_inverse):
        rows, columns = inverse_anc.shape
        width = diag_inverse.shape[1]
        planned = (
            n_col == 2 and n_row == 2 * FAR and rows == 2 * width
            and structure.shape[0] == 1 and columns == FAR * rows
        )
        if planned:
            return local_two(n_row, inverse_anc, lower_panel, structure, diag_inverse)
        return local_any(inverse_anc, lower_panel, structure, diag_inverse)

    return jax.shard_map(
        local,
        mesh=mesh,
        in_specs=(P("row", "col"), P("row", "col"), P("col", None), P("col", None)),
        out_specs=(P("row", "col"), P("col", None)),
        check_vma=False,
    )
```

```python
import functools

import jax
import jax.numpy as jnp
from jax import lax
from jax.experimental import pallas as pl
from jax.experimental.pallas import tpu as pltpu
from jax.sharding import PartitionSpec as P


BOTH = ("row", "col")


def keep_rows(structure, first_row, row_count, sn_width):
    block_ids = (first_row + jnp.arange(row_count, dtype=jnp.int32)) // sn_width
    listed = jnp.any(structure[None, :, :] == block_ids[:, None, None], axis=2)
    return jnp.repeat(listed, sn_width, axis=1)


def local_any(inverse_anc, lower_panel, structure, diag_inverse):
    local_rows = inverse_anc.shape[0]
    sn_width = diag_inverse.shape[1]
    local_count = structure.shape[0]
    keep = keep_rows(structure, lax.axis_index("row") * local_rows, local_rows, sn_width)
    masked = jnp.where(keep, lower_panel, jnp.float32(0.0))
    rows = lax.all_gather(masked, "row", axis=0, tiled=True)
    rows = lax.all_to_all(rows, "col", split_axis=0, concat_axis=1, tiled=True)
    part = jnp.dot(inverse_anc, rows, precision=lax.Precision.HIGHEST)
    product = lax.psum_scatter(part, "col", scatter_dimension=1, tiled=True)
    panel = jnp.where(keep, -product, jnp.float32(0.0))
    terms = jnp.einsum(
        "ika,ikb->kab",
        masked.reshape(local_rows, local_count, sn_width),
        panel.reshape(local_rows, local_count, sn_width),
        precision=lax.Precision.HIGHEST,
    )
    total = lax.psum(terms.reshape(local_count * sn_width, sn_width), "row")
    return panel, diag_inverse - total


def split(value):
    high = value.astype(jnp.bfloat16)
    low = (value - high.astype(jnp.float32)).astype(jnp.bfloat16)
    return high, low


def dot3(a, b, dims):
    dot = lambda u, v: lax.dot_general(u, v, (dims, ((), ())), preferred_element_type=jnp.float32)
    return dot(a[0], b[0]) + (dot(a[0], b[1]) + dot(a[1], b[0]))


def product_kernel(slots, blocks, width, mode, final, table, *refs):
    active = table[2 * len(slots) + blocks + 1] > 0

    @pl.when(active)
    def _():
        product_body(slots, blocks, width, mode, final, table, *refs)

    if mode == "keep":
        arrays = 1 + max(slot[0] for slot in slots)

        @pl.when(jnp.logical_not(active))
        def _():
            copy = pltpu.make_async_copy(refs[1 + arrays], refs[2 + arrays], refs[-1].at[0])
            copy.start()
            copy.wait()


def product_body(slots, blocks, width, mode, final, table, *refs):
    count = len(slots)
    narrays = 1 + max(s[0] for s in slots)
    refs = list(refs)
    a_hbm = refs.pop(0)
    arrays = [refs.pop(0) for _ in range(narrays)]
    acc_in = refs.pop(0) if mode else None
    has_acc = mode == "sum"
    extra_in = refs.pop(0) if final else None
    out = refs.pop(0)
    terms = refs.pop(0) if final else None
    a_buf, p_buf, extra, a_sem, p_sem, one_sem = refs
    row_on = [table[2 * count + rb] > 0 for rb in range(blocks)]
    all_on = functools.reduce(jnp.logical_and, row_on)
    dot = functools.partial(jnp.dot, preferred_element_type=jnp.float32)

    held = a_buf.shape[0]

    def a_copy(p, rb):
        return pltpu.make_async_copy(
            a_hbm.at[pl.ds(rb * width, width), pl.ds(pl.multiple_of(table[p] * width, width), width)],
            a_buf.at[p % held, rb],
            a_sem.at[p % held, rb],
        )

    def start(p):
        array, at = slots[p]

        @pl.when(table[count + p] > 0)
        def _():
            pltpu.make_async_copy(
                arrays[array].at[pl.ds(at * width, width), :], p_buf.at[p % held], p_sem.at[p % held]
            ).start()
            for rb in range(blocks):
                @pl.when(row_on[rb])
                def _(rb=rb):
                    a_copy(p, rb).start()

    if has_acc:
        acc_copy = pltpu.make_async_copy(acc_in, out, one_sem.at[0])
        acc_copy.start()
    for p in range(held):
        start(p)
    if final:
        extra_copy = pltpu.make_async_copy(extra_in, extra, one_sem.at[1])
        extra_copy.start()
    if has_acc:
        acc_copy.wait()
    else:
        out[...] = jnp.zeros_like(out)

    def step(p, carry):
        @pl.when(table[count + p] > 0)
        def _():
            slot = p % held
            pltpu.make_async_copy(p_buf.at[slot], p_buf.at[slot], p_sem.at[slot]).wait()
            high, low = split(p_buf[slot])

            def add(first, size):
                for rb in range(first, first + size):
                    a_copy(p, rb).wait()
                a_high, a_low = split(a_buf[slot, first : first + size].reshape(size * width, width))
                both = dot(jnp.concatenate([a_high, a_low]), high)
                total = both[: size * width] + (both[size * width :] + dot(a_high, low))
                out[pl.ds(first * width, size * width), :] += total

            @pl.when(all_on)
            def _():
                add(0, blocks)

            for rb in range(blocks):
                @pl.when(jnp.logical_not(all_on) & row_on[rb])
                def _(rb=rb):
                    add(rb, 1)

        for later in range(held, count):
            @pl.when(p == later - held)
            def _(later=later):
                start(later)

        return carry

    if count > 4:
        lax.fori_loop(0, count, step, 0)
    else:
        for p in range(count):
            step(p, 0)
    if final:
        extra_copy.wait()
        terms[...] = jnp.zeros_like(terms)
        for rb in range(blocks):
            rows = pl.ds(rb * width, width)

            @pl.when(row_on[rb])
            def _(rows=rows):
                terms[...] += dot3(split(extra[rows, :]), split(out[rows, :]), ((0,), (0,)))

        @pl.when(table[2 * count + blocks] > 0)
        def _():
            terms[...] += terms[...].T


def product(table, inverse_anc, arrays, slots, width, acc=None, extra=None, kind=jax.ShapeDtypeStruct, mode=None):
    rows = inverse_anc.shape[0]
    blocks = rows // width
    count = len(slots)
    held = count
    any_spec = pl.BlockSpec(memory_space=pl.ANY)
    vmem = pl.BlockSpec(memory_space=pltpu.VMEM)
    operands = [pltpu.with_memory_space_constraint(inverse_anc, pltpu.HBM), *arrays]
    specs = [pl.BlockSpec(memory_space=pltpu.HBM)] + [any_spec] * len(arrays)
    for more in (acc, extra):
        if more is not None:
            operands.append(more)
            specs.append(any_spec)
    shapes = [kind((rows, width), jnp.float32)]
    if extra is not None:
        shapes.append(jax.ShapeDtypeStruct((width, width), jnp.float32))
    return pl.pallas_call(
        functools.partial(product_kernel, slots, blocks, width, mode, extra is not None),
        out_shape=shapes,
        grid_spec=pltpu.PrefetchScalarGridSpec(
            num_scalar_prefetch=1,
            grid=(1,),
            in_specs=specs,
            out_specs=[vmem] * len(shapes),
            scratch_shapes=[
                pltpu.VMEM((held, blocks, width, width), jnp.float32),
                pltpu.VMEM((held, width, width), jnp.float32),
                pltpu.VMEM((rows, width), jnp.float32),
                pltpu.SemaphoreType.DMA((held, blocks)),
                pltpu.SemaphoreType.DMA((held,)),
                pltpu.SemaphoreType.DMA((2,)),
            ],
        ),
        compiler_params=pltpu.CompilerParams(vmem_limit_bytes=20 * 1024 * 1024),
        cost_estimate=pl.CostEstimate(
            flops=6 * rows * width * width * count // 4,
            bytes_accessed=4 * rows * width * count // 2,
            transcendentals=0,
        ),
    )(table, *operands)


CORE, X, Z, FAR = 1, 2, 4, 8
FIRST = tuple((m | c, h) for c in (0, 1) for m in (0, X, Z) for h in (0, 1))
SECOND = tuple((Z | X | c, h) for c in (0, 1) for h in (0, 1))
SLOTS1 = tuple((i, h) for i in range(6) for h in (0, 1))
SLOTS2 = tuple((i, 0) for i in range(4))
WHOLE = FIRST + tuple((Z | X | c, h) for c in (0, 1) for h in (0, 1))
SLOTSW = SLOTS1 + tuple((6 + i, h) for i in range(2) for h in (0, 1))
SLOTS12 = SLOTS1 + tuple((6 + i, 0) for i in range(4))


def local_two(n_row, inverse_anc, lower_panel, structure, diag_inverse):
    n_col = 2
    rows = inverse_anc.shape[0]
    width = diag_inverse.shape[1]
    half = rows // 2
    row, col = lax.axis_index("row"), lax.axis_index("col")
    near = (row // FAR) == col
    every = [(r, c) for r in range(n_row) for c in range(n_col)]

    def is_near(r, c):
        return r // FAR == c

    def move(value, mask, across, who=None):
        pairs = [
            (r * n_col + c, (r ^ mask) * n_col + (c ^ across))
            for r, c in every
            if who is None or is_near(r, c) == who
        ]
        return lax.ppermute(value, BOTH, pairs)

    def table(listed, order, who):
        block = ((row % FAR) ^ jnp.array([m for m, _ in order], jnp.int32)) * 2
        block = block + jnp.array([h for _, h in order], jnp.int32)
        ids = jnp.concatenate([block + col * 2 * FAR, row * 2 + jnp.arange(2, dtype=jnp.int32)])
        on = jnp.any(ids[:, None] == listed[0][None, :], axis=1)
        if who is not None:
            on = on & (near == who)
        far = jnp.logical_not(near) if who is None else jnp.zeros((), jnp.bool_)
        active = near == who if who is not None else jnp.ones((), jnp.bool_)
        flags = jnp.concatenate([on, far[None], active[None]])
        return jnp.concatenate([block, flags.astype(jnp.int32)])

    def step_one(q, who):
        return move(q, X, 0, who), move(q, Z, 0, who)

    def step_two(one, who):
        z2 = move(one[0][:half], Z, 0, who)
        return z2, move(one[1][half:], X, 0, who)

    def with_sibling(arrays, who):
        return list(arrays) + [move(v, CORE, 0, who) for v in arrays]

    other_structure = move(structure, 0, 1)
    got_far = move(lower_panel, FAR, 1, False)
    lower_other = move(lower_panel, 0, 1)
    n_one = step_one(lower_panel, True)
    q_far = move(lower_panel, FAR, 0, True)
    n_two = step_two(n_one, True)
    in_hbm = lambda v: pltpu.with_memory_space_constraint(v, pltpu.HBM)
    n_first = with_sibling([lower_panel, *n_one], None)
    n_first[0] = in_hbm(lower_panel)
    n_second = with_sibling(n_two, None)
    q_other = jnp.where(near, lower_other, got_far)
    o_one = step_one(q_other, None)
    o_two = step_two(o_one, None)
    o_first = with_sibling([q_other, *o_one], None)
    o_second = with_sibling(o_two, None)
    f_one = step_one(q_far, False)
    f_two = [move(q_far, Z | X, 0, False)]
    f_first = with_sibling([q_far, *f_one], None)
    f_second = with_sibling(f_two, None)

    own, own_terms = product(
        table(structure, FIRST + SECOND, True), inverse_anc, n_first + n_second, SLOTS12, width,
        extra=n_first[0], kind=pltpu.HBM,
    )
    (part,) = product(table(other_structure, FIRST, None), inverse_anc, o_first, SLOTS1, width)
    part, other_terms = product(
        table(other_structure, SECOND, None), inverse_anc, o_second, SLOTS2, width,
        acc=part, extra=lower_other, kind=pltpu.HBM, mode="sum",
    )
    recv = move(part, 0, 1)
    (own,) = product(
        table(structure, WHOLE, False), inverse_anc, f_first + f_second, SLOTSW, width,
        acc=in_hbm(own), mode="keep",
    )
    keep = keep_rows(structure, row * rows, rows, width)
    panel = jnp.where(keep, -(own + recv), jnp.float32(0.0))

    def parts(value, mask):
        size = value.shape[0] // 2
        bit = (row & mask) > 0
        low, high = value[:size], value[size:]
        return jnp.where(bit, high, low), jnp.where(bit, low, high)

    def double(value, mask):
        bit = (row & mask) > 0
        got = move(value, mask, 0)
        return jnp.concatenate([jnp.where(bit, got, value), jnp.where(bit, value, got)])

    u_keep, u_send = parts(jnp.where(near, own_terms, jnp.float32(0.0)), CORE)
    v_keep, v_send = parts(other_terms, CORE)
    size = u_keep.shape[0]
    got = move(jnp.concatenate([u_send, v_send]), CORE, 0)
    u_keep, u_send = parts(u_keep + got[:size], X)
    v_keep, v_send = parts(v_keep + got[size:], X)
    total = u_keep + move(u_send, X, 0) + move(v_keep, 0, 1) + move(v_send, X, 1)
    total = total + move(total, Z, 0) + move(total, FAR, 0) + move(total, FAR | Z, 0)
    total = double(double(total, X), CORE)
    return panel, diag_inverse + total


def solution(mesh):
    n_row, n_col = mesh.shape["row"], mesh.shape["col"]

    def local(inverse_anc, lower_panel, structure, diag_inverse):
        rows, columns = inverse_anc.shape
        width = diag_inverse.shape[1]
        planned = (
            n_col == 2 and n_row == 2 * FAR and rows == 2 * width
            and structure.shape[0] == 1 and columns == FAR * rows
        )
        if planned:
            return local_two(n_row, inverse_anc, lower_panel, structure, diag_inverse)
        return local_any(inverse_anc, lower_panel, structure, diag_inverse)

    return jax.shard_map(
        local,
        mesh=mesh,
        in_specs=(P("row", "col"), P("row", "col"), P("col", None), P("col", None)),
        out_specs=(P("row", "col"), P("col", None)),
        check_vma=False,
    )
```

```python
import functools

import jax
import jax.numpy as jnp
from jax import lax
from jax.experimental import pallas as pl
from jax.experimental.pallas import tpu as pltpu
from jax.sharding import PartitionSpec as P


BOTH = ("row", "col")


def keep_rows(structure, first_row, row_count, sn_width):
    block_ids = (first_row + jnp.arange(row_count, dtype=jnp.int32)) // sn_width
    listed = jnp.any(structure[None, :, :] == block_ids[:, None, None], axis=2)
    return jnp.repeat(listed, sn_width, axis=1)


def local_any(inverse_anc, lower_panel, structure, diag_inverse):
    local_rows = inverse_anc.shape[0]
    sn_width = diag_inverse.shape[1]
    local_count = structure.shape[0]
    keep = keep_rows(structure, lax.axis_index("row") * local_rows, local_rows, sn_width)
    masked = jnp.where(keep, lower_panel, jnp.float32(0.0))
    rows = lax.all_gather(masked, "row", axis=0, tiled=True)
    rows = lax.all_to_all(rows, "col", split_axis=0, concat_axis=1, tiled=True)
    part = jnp.dot(inverse_anc, rows, precision=lax.Precision.HIGHEST)
    product = lax.psum_scatter(part, "col", scatter_dimension=1, tiled=True)
    panel = jnp.where(keep, -product, jnp.float32(0.0))
    terms = jnp.einsum(
        "ika,ikb->kab",
        masked.reshape(local_rows, local_count, sn_width),
        panel.reshape(local_rows, local_count, sn_width),
        precision=lax.Precision.HIGHEST,
    )
    total = lax.psum(terms.reshape(local_count * sn_width, sn_width), "row")
    return panel, diag_inverse - total


def split(value):
    high = value.astype(jnp.bfloat16)
    low = (value - high.astype(jnp.float32)).astype(jnp.bfloat16)
    return high, low


def dot3(a, b, dims):
    dot = lambda u, v: lax.dot_general(u, v, (dims, ((), ())), preferred_element_type=jnp.float32)
    return dot(a[0], b[0]) + (dot(a[0], b[1]) + dot(a[1], b[0]))


def product_kernel(slots, blocks, width, mode, final, table, *refs):
    active = table[2 * len(slots) + blocks + 1] > 0

    @pl.when(active)
    def _():
        product_body(slots, blocks, width, mode, final, table, *refs)

    if mode == "keep":
        arrays = 1 + max(slot[0] for slot in slots)

        @pl.when(jnp.logical_not(active))
        def _():
            copy = pltpu.make_async_copy(refs[1 + arrays], refs[2 + arrays], refs[-1].at[0])
            copy.start()
            copy.wait()


def product_body(slots, blocks, width, mode, final, table, *refs):
    count = len(slots)
    narrays = 1 + max(s[0] for s in slots)
    refs = list(refs)
    a_hbm = refs.pop(0)
    arrays = [refs.pop(0) for _ in range(narrays)]
    acc_in = refs.pop(0) if mode else None
    has_acc = mode == "sum"
    extra_in = refs.pop(0) if final else None
    out = refs.pop(0)
    terms = refs.pop(0) if final == "terms" else None
    a_buf, p_buf, extra, a_sem, p_sem, one_sem = refs
    row_on = [table[2 * count + rb] > 0 for rb in range(blocks)]
    all_on = functools.reduce(jnp.logical_and, row_on)
    dot = functools.partial(jnp.dot, preferred_element_type=jnp.float32)

    held = a_buf.shape[0]

    def a_copy(p, rb):
        return pltpu.make_async_copy(
            a_hbm.at[pl.ds(rb * width, width), pl.ds(pl.multiple_of(table[p] * width, width), width)],
            a_buf.at[p % held, rb],
            a_sem.at[p % held, rb],
        )

    def start(p):
        array, at = slots[p]

        @pl.when(table[count + p] > 0)
        def _():
            pltpu.make_async_copy(
                arrays[array].at[pl.ds(at * width, width), :], p_buf.at[p % held], p_sem.at[p % held]
            ).start()
            for rb in range(blocks):
                @pl.when(row_on[rb])
                def _(rb=rb):
                    a_copy(p, rb).start()

    if has_acc:
        acc_copy = pltpu.make_async_copy(acc_in, out, one_sem.at[0])
        acc_copy.start()
    for p in range(held):
        start(p)
    if final:
        extra_copy = pltpu.make_async_copy(extra_in, extra, one_sem.at[1])
        extra_copy.start()
    if has_acc:
        acc_copy.wait()
    else:
        out[...] = jnp.zeros_like(out)

    def step(p, carry):
        @pl.when(table[count + p] > 0)
        def _():
            slot = p % held
            pltpu.make_async_copy(p_buf.at[slot], p_buf.at[slot], p_sem.at[slot]).wait()
            high, low = split(p_buf[slot])

            def add(first, size):
                for rb in range(first, first + size):
                    a_copy(p, rb).wait()
                a_high, a_low = split(a_buf[slot, first : first + size].reshape(size * width, width))
                both = dot(jnp.concatenate([a_high, a_low]), high)
                total = both[: size * width] + (both[size * width :] + dot(a_high, low))
                out[pl.ds(first * width, size * width), :] += total

            @pl.when(all_on)
            def _():
                add(0, blocks)

            for rb in range(blocks):
                @pl.when(jnp.logical_not(all_on) & row_on[rb])
                def _(rb=rb):
                    add(rb, 1)

        for later in range(held, count):
            @pl.when(p == later - held)
            def _(later=later):
                start(later)

        return carry

    if count > 4:
        lax.fori_loop(0, count, step, 0)
    else:
        for p in range(count):
            step(p, 0)
    if final:
        extra_copy.wait()
    if final == "panel":
        for rb in range(blocks):
            rows = pl.ds(rb * width, width)
            out[rows, :] = jnp.where(row_on[rb], -(out[rows, :] + extra[rows, :]), jnp.float32(0.0))
    if final == "terms":
        terms[...] = jnp.zeros_like(terms)
        for rb in range(blocks):
            rows = pl.ds(rb * width, width)

            @pl.when(row_on[rb])
            def _(rows=rows):
                terms[...] += dot3(split(extra[rows, :]), split(out[rows, :]), ((0,), (0,)))

        @pl.when(table[2 * count + blocks] > 0)
        def _():
            terms[...] += terms[...].T


def product(table, inverse_anc, arrays, slots, width, acc=None, extra=None, kind=jax.ShapeDtypeStruct, mode=None, final=None):
    rows = inverse_anc.shape[0]
    blocks = rows // width
    count = len(slots)
    held = count
    any_spec = pl.BlockSpec(memory_space=pl.ANY)
    vmem = pl.BlockSpec(memory_space=pltpu.VMEM)
    operands = [pltpu.with_memory_space_constraint(inverse_anc, pltpu.HBM), *arrays]
    specs = [pl.BlockSpec(memory_space=pltpu.HBM)] + [any_spec] * len(arrays)
    for more in (acc, extra):
        if more is not None:
            operands.append(more)
            specs.append(any_spec)
    shapes = [kind((rows, width), jnp.float32)]
    if final == "terms":
        shapes.append(jax.ShapeDtypeStruct((width, width), jnp.float32))
    return pl.pallas_call(
        functools.partial(product_kernel, slots, blocks, width, mode, final),
        out_shape=shapes,
        grid_spec=pltpu.PrefetchScalarGridSpec(
            num_scalar_prefetch=1,
            grid=(1,),
            in_specs=specs,
            out_specs=[vmem] * len(shapes),
            scratch_shapes=[
                pltpu.VMEM((held, blocks, width, width), jnp.float32),
                pltpu.VMEM((held, width, width), jnp.float32),
                pltpu.VMEM((rows, width), jnp.float32),
                pltpu.SemaphoreType.DMA((held, blocks)),
                pltpu.SemaphoreType.DMA((held,)),
                pltpu.SemaphoreType.DMA((2,)),
            ],
        ),
        compiler_params=pltpu.CompilerParams(vmem_limit_bytes=20 * 1024 * 1024),
        cost_estimate=pl.CostEstimate(
            flops=6 * rows * width * width * count // 4,
            bytes_accessed=4 * rows * width * count // 2,
            transcendentals=0,
        ),
    )(table, *operands)


CORE, X, Z, FAR = 1, 2, 4, 8
FIRST = tuple((m | c, h) for c in (0, 1) for m in (0, X, Z) for h in (0, 1))
SECOND = tuple((Z | X | c, h) for c in (0, 1) for h in (0, 1))
SLOTS1 = tuple((i, h) for i in range(6) for h in (0, 1))
SLOTS2 = tuple((i, 0) for i in range(4))
SLOTS2B = tuple((i, h) for i in range(2) for h in (0, 1))


def local_two(n_row, inverse_anc, lower_panel, structure, diag_inverse):
    n_col = 2
    rows = inverse_anc.shape[0]
    width = diag_inverse.shape[1]
    half = rows // 2
    row, col = lax.axis_index("row"), lax.axis_index("col")
    near = (row // FAR) == col
    every = [(r, c) for r in range(n_row) for c in range(n_col)]

    def is_near(r, c):
        return r // FAR == c

    def move(value, mask, across, who=None):
        pairs = [
            (r * n_col + c, (r ^ mask) * n_col + (c ^ across))
            for r, c in every
            if who is None or is_near(r, c) == who
        ]
        return lax.ppermute(value, BOTH, pairs)

    def table(listed, order, who, everywhere=False):
        block = ((row % FAR) ^ jnp.array([m for m, _ in order], jnp.int32)) * 2
        block = block + jnp.array([h for _, h in order], jnp.int32)
        ids = jnp.concatenate([block + col * 2 * FAR, row * 2 + jnp.arange(2, dtype=jnp.int32)])
        on = jnp.any(ids[:, None] == listed[0][None, :], axis=1)
        count = len(order)
        if who is not None:
            served = (near == who) | (everywhere & (jnp.arange(count + 2) >= count))
            on = on & served
        far = jnp.logical_not(near) & jnp.bool_(who is None and order == SECOND)
        active = near == who if who is not None and not everywhere else jnp.ones((), jnp.bool_)
        flags = jnp.concatenate([on, far[None], active[None]])
        return jnp.concatenate([block, flags.astype(jnp.int32)])

    def step_one(q, who):
        return move(q, X, 0, who), move(q, Z, 0, who)

    def step_two(one, who):
        z2 = move(one[0][:half], Z, 0, who)
        return z2, move(one[1][half:], X, 0, who)

    def with_sibling(arrays, who):
        return list(arrays) + [move(v, CORE, 0, who) for v in arrays]

    other_structure = move(structure, 0, 1)
    got_far = move(lower_panel, FAR, 1, False)
    lower_other = move(lower_panel, 0, 1)
    n_one = step_one(lower_panel, True)
    q_far = move(lower_panel, FAR, 0, True)
    n_two = step_two(n_one, True)
    in_hbm = lambda v: pltpu.with_memory_space_constraint(v, pltpu.HBM)
    n_first = with_sibling([lower_panel, *n_one], None)
    n_first[0] = in_hbm(lower_panel)
    n_second = with_sibling(n_two, None)
    q_other = jnp.where(near, lower_other, got_far)
    o_one = step_one(q_other, None)
    other_structure, _ = lax.optimization_barrier((other_structure, o_one[0]))
    o_two = step_two(o_one, None)
    o_first = with_sibling([q_other, *o_one], None)
    o_second = with_sibling(o_two, None)
    f_one = step_one(q_far, False)
    f_two = [move(q_far, Z | X, 0, False)]
    f_first = with_sibling([q_far, *f_one], None)
    f_second = with_sibling(f_two, None)

    (own,) = product(table(structure, FIRST, True), inverse_anc, n_first, SLOTS1, width)
    (part,) = product(table(other_structure, FIRST, None), inverse_anc, o_first, SLOTS1, width)
    own, part = lax.optimization_barrier((own, part))
    own, own_terms = product(
        table(structure, SECOND, True), inverse_anc, n_second, SLOTS2, width,
        acc=own, extra=n_first[0], kind=pltpu.HBM, mode="sum", final="terms",
    )
    part, other_terms = product(
        table(other_structure, SECOND, None), inverse_anc, o_second, SLOTS2, width,
        acc=part, extra=lower_other, kind=pltpu.HBM, mode="sum", final="terms",
    )
    recv = move(part, 0, 1)
    (own,) = product(
        table(structure, FIRST, False), inverse_anc, f_first, SLOTS1, width,
        acc=in_hbm(own), mode="keep",
    )
    (panel,) = product(
        table(structure, SECOND, False, True), inverse_anc, f_second, SLOTS2B, width,
        acc=own, extra=recv, mode="sum", final="panel",
    )

    def parts(value, mask):
        size = value.shape[0] // 2
        bit = (row & mask) > 0
        low, high = value[:size], value[size:]
        return jnp.where(bit, high, low), jnp.where(bit, low, high)

    def double(value, mask):
        bit = (row & mask) > 0
        got = move(value, mask, 0)
        return jnp.concatenate([jnp.where(bit, got, value), jnp.where(bit, value, got)])

    u_keep, u_send = parts(jnp.where(near, own_terms, jnp.float32(0.0)), CORE)
    v_keep, v_send = parts(other_terms, CORE)
    size = u_keep.shape[0]
    got = move(jnp.concatenate([u_send, v_send]), CORE, 0)
    u_keep, u_send = parts(u_keep + got[:size], X)
    v_keep, v_send = parts(v_keep + got[size:], X)
    total = u_keep + move(u_send, X, 0) + move(v_keep, 0, 1) + move(v_send, X, 1)
    total = total + move(total, Z, 0) + move(total, FAR, 0) + move(total, FAR | Z, 0)
    total = double(double(total, X), CORE)
    return panel, diag_inverse + total


def solution(mesh):
    n_row, n_col = mesh.shape["row"], mesh.shape["col"]

    def local(inverse_anc, lower_panel, structure, diag_inverse):
        rows, columns = inverse_anc.shape
        width = diag_inverse.shape[1]
        planned = (
            n_col == 2 and n_row == 2 * FAR and rows == 2 * width
            and structure.shape[0] == 1 and columns == FAR * rows
        )
        if planned:
            return local_two(n_row, inverse_anc, lower_panel, structure, diag_inverse)
        return local_any(inverse_anc, lower_panel, structure, diag_inverse)

    return jax.shard_map(
        local,
        mesh=mesh,
        in_specs=(P("row", "col"), P("row", "col"), P("col", None), P("col", None)),
        out_specs=(P("row", "col"), P("col", None)),
        check_vma=False,
    )
```
